256 devices in a mesh: leaf: 64 (over z, y, core), sub: 4 (over x).
Axes of the slice: x: 4, y: 4, z: 8, core: 2. Of those that a mesh axis runs over, the one named last changes fastest.
Arguments:
- sources: bfloat16 [524288, 64], P(('leaf', 'sub')), may hold values from -6 to 6
- leaf_basis: bfloat16 [2048, 256, 64], P(('leaf', 'sub')), may hold values from -0.375 to 0.375
- transfer: float32 [2, 64, 64], replicated, may hold values from -0.625 to 0.625
- coupling: float32 [3, 64, 64], replicated, may hold values from -0.5 to 0.5
- near_blocks: bfloat16 [2048, 4, 256, 256], P(('leaf', 'sub')), may hold values from -0.1875 to 0.1875
- near_pattern: int32 [2048, 4], P(('leaf', 'sub')), may hold values from 0 to 2047, as said below
- far_pattern: int32 [4092, 3], replicated, may hold values 0 or 1
Outputs:
- product: bfloat16 [524288, 64], P(('leaf', 'sub'))
The draws below stay inside these ranges and needn't reach their ends.
Inputs may be any that keep to these rules, and one draw needn't show every extreme that they name: near_pattern[i, 0] = i; every entry j has j // 8 - i // 8 equal to 0, 1, -1, 4 or -4.
All inputs are finite; a program needn't handle non-finite values.
Results may differ from the reference program's by a relative error of at most 0.001.
Values may be sent and summed in bfloat16 or wider, within the bound.
No kernel may reach another device: no remote copies, remote signals or barrier semaphores. Data moves between devices by JAX's collectives and lax.ppermute only.
A program may use at most 64 MiB of HBM per device.

```python
import jax
import jax.numpy as jnp
from jax import lax

LEAF_PTS = 256
RANK = 64
RHS = 64
NEAR = 4
LEAF_DEV = 8
SUB_SPAN = 4
LEAVES = 2048
POINTS = 524288
FAR_ROWS = 4092


def draw_near_pattern(key, part):
    leaf_ids = jnp.arange(LEAVES, dtype=jnp.int32)
    device_ids = leaf_ids // LEAF_DEV
    device_total = LEAVES // LEAF_DEV
    key_side, key_leaf = jax.random.split(jax.random.fold_in(key, 17))
    direction = jax.random.randint(key_side, (LEAVES, NEAR), 0, 5)
    steps_table = jnp.array([0, -1, 1, -SUB_SPAN, SUB_SPAN], jnp.int32)
    target = device_ids[:, None] + steps_table[direction]
    target = jnp.where((target < 0) | (target >= device_total), device_ids[:, None], target)
    within = jax.random.randint(key_leaf, (LEAVES, NEAR), 0, LEAF_DEV)
    chosen = (target * LEAF_DEV + within).astype(jnp.int32)
    return chosen.at[:, 0].set(leaf_ids)


def touch_ends(values, stream_key, smallest, top_value):
    shape = values.shape
    place = [jax.random.randint(jax.random.fold_in(stream_key, axis), (), 0, shape[axis]) for axis in range(len(shape))]
    values = values.at[tuple(place)].set(smallest)
    longest = shape.index(max(shape))
    place[longest] = (place[longest] + 1) % shape[longest]
    return values.at[tuple(place)].set(top_value)


def levels(own_key, dims, cuts, smallest, largest):
    factor_of, own = 1.0, jax.random.fold_in(own_key, 6)
    for position, blocks in cuts:
        heights = jnp.exp(jax.random.uniform(jax.random.fold_in(own, position), (blocks,), jnp.float32, smallest / len(cuts), largest / len(cuts)))
        factor_of = factor_of * jnp.repeat(heights, dims[position] // blocks).reshape([-1 if axis == position else 1 for axis in range(len(dims))])
    return factor_of


def centred(stream_key, shape, scale, bound, cuts=(), kind=jnp.bfloat16):
    values = scale * jax.random.normal(stream_key, shape, jnp.float32)
    if cuts:
        values = values * levels(stream_key, shape, cuts, -0.22, 0.18)
    return jnp.clip(values, -bound, bound).astype(kind)


def setup_inputs(seed: int = 0) -> dict:
    keys = jax.random.split(jax.random.key(seed), 8)
    return {
        "sources": centred(keys[0], (POINTS, RHS), 1.0, 6.0, ((0, 256),)),
        "leaf_basis": centred(keys[1], (LEAVES, LEAF_PTS, RANK), LEAF_PTS ** -0.5, 0.375, ((0, 256),)),
        "transfer": centred(keys[2], (2, RANK, RANK), (3 * RANK // 2) ** -0.5, 0.625, (), jnp.float32),
        "coupling": centred(keys[3], (3, RANK, RANK), (2 * RANK) ** -0.5, 0.5, (), jnp.float32),
        "near_blocks": centred(keys[4], (LEAVES, NEAR, LEAF_PTS, LEAF_PTS), (NEAR * LEAF_PTS) ** -0.5, 0.1875, ((0, 256),)),
        "near_pattern": draw_near_pattern(jax.random.fold_in(keys[7], 71), 0),
        "far_pattern": touch_ends((jax.random.randint(keys[6], (FAR_ROWS, 3), 0, 3) < 2).astype(jnp.int32), jax.random.fold_in(keys[6], 1), 0, 1),
    }


PRECISE = lax.Precision.HIGHEST


def lift_up(level_vals, transfer):
    paired = level_vals.reshape(-1, 2, level_vals.shape[1], level_vals.shape[2])
    left_part = jnp.einsum('jk,pjr->pkr', transfer[0], paired[:, 0], precision=PRECISE)
    right_part = jnp.einsum('jk,pjr->pkr', transfer[1], paired[:, 1], precision=PRECISE)
    return left_part + right_part


def expand_down(parent_field, transfer):
    first_child = jnp.einsum('kj,pjr->pkr', transfer[0], parent_field, precision=PRECISE)
    second_child = jnp.einsum('kj,pjr->pkr', transfer[1], parent_field, precision=PRECISE)
    stacked = jnp.stack([first_child, second_child], 1)
    return stacked.reshape(-1, parent_field.shape[1], parent_field.shape[2])


def couple_level(level_vals, mask_rows, coupling):
    grouped = level_vals.reshape(-1, 4, level_vals.shape[1], level_vals.shape[2])
    summed = jnp.zeros(level_vals.shape, jnp.float32)
    for offset in range(1, 4):
        shifted = jnp.roll(grouped, -offset, axis=1).reshape(level_vals.shape)
        product_term = jnp.einsum('ab,nbr->nar', coupling[offset - 1], shifted, precision=PRECISE)
        weights = mask_rows[:, offset - 1:offset].astype(jnp.float32)[:, :, None]
        summed = summed + weights * product_term
    return summed


def reference(sources, leaf_basis, transfer, coupling, near_blocks, near_pattern, far_pattern):
    leaf_count = leaf_basis.shape[0]
    points = sources.reshape(leaf_count, LEAF_PTS, RHS).astype(jnp.float32)
    basis_wide = leaf_basis.astype(jnp.float32)
    moments = [jnp.einsum('lpk,lpr->lkr', basis_wide, points, precision=PRECISE)]
    while moments[-1].shape[0] > 4:
        moments.append(lift_up(moments[-1], transfer))
    locals_list = []
    row_start = 0
    for level_vals in moments:
        cluster_count = level_vals.shape[0]
        mask_rows = far_pattern[row_start:row_start + cluster_count]
        locals_list.append(couple_level(level_vals, mask_rows, coupling))
        row_start = row_start + cluster_count
    field_down = locals_list[-1]
    for level_id in range(len(moments) - 2, -1, -1):
        field_down = locals_list[level_id] + expand_down(field_down, transfer)
    far_part = jnp.einsum('lpk,lkr->lpr', basis_wide, field_down, precision=PRECISE)
    device_total = leaf_count // LEAF_DEV
    blocks_grouped = near_blocks.reshape(device_total, LEAF_DEV, NEAR, LEAF_PTS, LEAF_PTS)
    pattern_grouped = near_pattern.reshape(device_total, LEAF_DEV, NEAR)

    def near_one(inputs):
        blocks_here, pattern_here = inputs
        gathered = points[pattern_here]
        return jnp.einsum('lsab,lsbr->lar', blocks_here.astype(jnp.float32), gathered, precision=PRECISE)

    near_part = lax.map(near_one, (blocks_grouped, pattern_grouped)).reshape(leaf_count, LEAF_PTS, RHS)
    return (far_part + near_part).reshape(leaf_count * LEAF_PTS, RHS).astype(jnp.bfloat16)
```

```python
import jax
import jax.numpy as jnp
from jax import lax
from jax.experimental import pallas as pl
from jax.experimental.pallas import tpu as pltpu
from jax.sharding import Mesh, PartitionSpec as P

AXES = ("z", "y", "c", "x")
F32 = jnp.float32
BF16 = jnp.bfloat16
NN = (((1,), (0,)), ((), ()))
NT = (((1,), (1,)), ((), ()))
VMEM = pl.BlockSpec(memory_space=pltpu.VMEM)
SMEM = pl.BlockSpec(memory_space=pltpu.SMEM)


def split(a):
    high = a.astype(BF16)
    return high, (a - high.astype(F32)).astype(BF16)


def dot(a, b, dims):
    return lax.dot_general(a, b, dims, preferred_element_type=F32)


def dot3(a, b, dims):
    return dot(a[0], b[0], dims) + (dot(a[0], b[1], dims) + dot(a[1], b[0], dims))


def lift(first, second, transfer):
    return dot3(split(first), transfer[0], NN) + dot3(split(second), transfer[1], NN)


def pair_of(first, second):
    return jnp.concatenate([first, second], axis=1)


def device_index():
    z, y, c, x = (lax.axis_index(a) for a in AXES)
    return ((z * lax.axis_size("y") + y) * lax.axis_size("c") + c) * lax.axis_size("x") + x


def swap(array, mask):
    count = 1
    for a in AXES:
        count *= lax.axis_size(a)
    return lax.ppermute(array, AXES, [(i, i ^ mask) for i in range(count)])


def ring(array, step):
    count = 1
    for a in AXES:
        count *= lax.axis_size(a)
    return lax.ppermute(array, AXES, [(i, (i + step) % count) for i in range(count)])


def leaf_kernel(src, basis, transfer, m0, m1, pair2):
    t = [split(transfer[i]) for i in range(2)]
    leaves = basis.shape[0]
    pts = basis.shape[2]
    low = []
    for i in range(leaves):
        v = dot(src[:, i * pts : (i + 1) * pts], basis[i], NT)
        m0[i] = v
        low.append(v)
    mid = [lift(low[2 * i], low[2 * i + 1], t) for i in range(leaves // 2)]
    for i, v in enumerate(mid):
        m1[i] = v
    pair2[...] = pair_of(lift(mid[0], mid[1], t), lift(mid[2], mid[3], t))


def clusters(pairs, out):
    for i, p in enumerate(pairs):
        out[2 * i] = p[:, :64]
        out[2 * i + 1] = p[:, 64:]


def up4_kernel(copies, here, own, p1, p2, p3, transfer, a, b, pair, ordered):
    t = [split(transfer[i]) for i in range(2)]
    for i, ref in enumerate((own, p1, p2, p3)):
        ordered[here[0] ^ i] = ref[...]
    pairs = [ordered[i] for i in range(4)]
    clusters(pairs, a)
    low = [a[i] for i in range(8)]
    mid = [lift(low[2 * i], low[2 * i + 1], t) for i in range(4)]
    for i, v in enumerate(mid):
        b[i] = v
    top = pair_of(lift(mid[0], mid[1], t), lift(mid[2], mid[3], t))
    if copies:
        for i in range(copies):
            pair[i] = top
    else:
        pair[...] = top


def up2_kernel(here, own, p1, transfer, a, pair, ordered):
    t = [split(transfer[i]) for i in range(2)]
    for i, ref in enumerate((own, p1)):
        ordered[here[0] ^ i] = ref[...]
    clusters([ordered[i] for i in range(2)], a)
    pair[...] = pair_of(lift(a[0], a[1], t), lift(a[2], a[3], t))


def near_kernel(place, own, after, before, up, down, blocks, out, held):
    leaves = held.shape[0] // 5
    pts = held.shape[2]

    @pl.when(pl.program_id(0) == 0)
    def _():
        for n, ref in enumerate((own, after, before, up, down)):
            for i in range(leaves):
                held[n * leaves + i] = ref[:, i * pts : (i + 1) * pts]

    leaf = pl.program_id(0)
    total = None
    for s in range(blocks.shape[1]):
        term = dot(held[place[s, leaf]], blocks[0, s], NT)
        total = term if total is None else total + term
    out[...] = total


def couple(weights, sources, coupling):
    total = None
    for w, m, c in zip(weights, sources, coupling):
        term = dot3(split(m * w), c, NT)
        total = term if total is None else total + term
    return total


def last_kernel(me, far, transfer, coupling, basis, m0, m1, m2, m3, m4, m5, m6, g7, near, out, m7, m8, m9):
    t = [split(transfer[i]) for i in range(2)]
    c = [split(coupling[i]) for i in range(3)]
    d = me[0]
    clusters([g7[i] for i in range(8)], m7)
    for i in range(8):
        m8[i] = lift(m7[2 * i], m7[2 * i + 1], t)
    for i in range(4):
        m9[i] = lift(m8[2 * i], m8[2 * i + 1], t)

    total_rows = far.shape[1]
    lane = lax.broadcasted_iota(jnp.int32, (3, 128), 1)

    def weights_of(row):
        base = row // 128 * 128
        chunk = far[:, pl.ds(pl.multiple_of(base, 128), 128)]
        return jnp.sum(jnp.where(lane == row - base, chunk, 0), axis=1, keepdims=True).astype(F32)

    tail = total_rows // 128 * 128
    tail_lane = lax.broadcasted_iota(jnp.int32, (3, total_rows - tail), 1)

    def tail_weights(row):
        return jnp.sum(jnp.where(tail_lane == row - tail, far[:, tail:], 0), axis=1, keepdims=True).astype(F32)

    starts = [0]
    for level in range(9):
        starts.append(starts[-1] + (2048 >> level))

    def local(level, cluster, values, width):
        row = starts[level] + cluster
        w = tail_weights(row) if starts[level] >= tail else weights_of(row)
        at = cluster % width
        group = at // 4 * 4
        sources = [values[group + (at + j) % 4] for j in (1, 2, 3)]
        return couple([w[j : j + 1, :] for j in range(3)], sources, c)

    field = local(9, d >> 6, m9, 4)
    for level, values, width in ((8, m8, 8), (7, m7, 16), (6, m6, 4), (5, m5, 8), (4, m4, 4), (3, m3, 4)):
        cluster = d >> (level - 3)
        child = cluster % 2
        one = split(transfer[child])
        field = local(level, cluster, values, width) + dot3(split(field), one, NT)
    parents = [field]
    for level, values, width, count in ((2, m2, 8, 2), (1, m1, 4, 4), (0, m0, 8, 8)):
        below = []
        for i in range(count):
            if level == 2:
                own = local(level, d * count + i, values, width)
            else:
                row = starts[level] + d * count + i
                w = weights_of(row)
                group = i // 4 * 4
                own = couple([w[j : j + 1, :] for j in range(3)], [values[group + (i + j + 1) % 4] for j in range(3)], c)
            below.append(own + dot3(split(parents[i // 2]), t[i % 2], NT))
        parents = below
    pts = basis.shape[2]
    for i, f in enumerate(parents):
        high, low = split(f)
        part = dot(high, basis[i], NN) + dot(low, basis[i], NN)
        at = slice(i * pts, (i + 1) * pts)
        out[:, at] = (part + near[:, at]).astype(BF16)


def shards(sources, leaf_basis, transfer, coupling, near_blocks, near_pattern, far_pattern):
    leaves, pts, rank = leaf_basis.shape
    rhs = sources.shape[1]
    d = device_index()
    src = sources.T
    basis = jnp.swapaxes(leaf_basis, 1, 2)
    mat = lambda n: jax.ShapeDtypeStruct((n, rhs, rank), F32)
    pair = jax.ShapeDtypeStruct((rhs, 2 * rank), F32)
    params = pltpu.CompilerParams(vmem_limit_bytes=40 * 1024 * 1024)

    after, before = ring(src, -1), ring(src, 1)
    up, down = ring(src, -4), ring(src, 4)

    m0, m1, pair2 = pl.pallas_call(
        leaf_kernel, out_shape=(mat(8), mat(4), pair), in_specs=[VMEM] * 3, out_specs=(VMEM,) * 3,
        name="leaf", compiler_params=params,
    )(src, basis, transfer)

    def up4(own, masks, here, copies):
        got = [swap(own, m) for m in masks]
        top = jax.ShapeDtypeStruct((copies,) + pair.shape, F32) if copies else pair
        return pl.pallas_call(
            lambda *refs: up4_kernel(copies, *refs),
            out_shape=(mat(8), mat(4), top), in_specs=[SMEM] + [VMEM] * 5, out_specs=(VMEM,) * 3,
            scratch_shapes=[pltpu.VMEM((4,) + pair.shape, F32)], name="up4", compiler_params=params,
        )(here.reshape(1), own, *got, transfer)

    m2, m3, pair4 = up4(pair2, (1, 2, 3), lax.axis_index("x"), 0)
    m4, pair5 = pl.pallas_call(
        up2_kernel, out_shape=(mat(4), pair), in_specs=[SMEM] + [VMEM] * 3, out_specs=(VMEM,) * 2,
        scratch_shapes=[pltpu.VMEM((2,) + pair.shape, F32)], name="up2", compiler_params=params,
    )(lax.axis_index("c").reshape(1), pair4, swap(pair4, 4), transfer)
    m5, m6, pair7 = up4(pair5, (8, 16, 24), lax.axis_index("y"), 8)
    g7 = lax.all_to_all(pair7, "z", 0, 0, tiled=True)

    gap = near_pattern.T // leaves - d
    slot = jnp.where(gap == 0, 0, jnp.where(gap == 1, 1, jnp.where(gap == -1, 2, jnp.where(gap == 4, 3, 4))))
    place = slot * leaves + near_pattern.T % leaves
    whole = lambda a: pl.BlockSpec(a.shape, lambda i, *_: (0,) * len(a.shape))
    near = pl.pallas_call(
        near_kernel,
        out_shape=jax.ShapeDtypeStruct((rhs, leaves * pts), F32),
        grid_spec=pltpu.PrefetchScalarGridSpec(
            num_scalar_prefetch=1,
            grid=(leaves,),
            in_specs=[whole(src)] * 5
            + [pl.BlockSpec((1,) + near_blocks.shape[1:], lambda i, *_: (i, 0, 0, 0))],
            out_specs=pl.BlockSpec((rhs, pts), lambda i, *_: (0, i)),
            scratch_shapes=[pltpu.VMEM((5 * leaves, rhs, pts), BF16)],
        ),
        name="near",
        compiler_params=params,
    )(place, src, after, before, up, down, near_blocks)

    product = pl.pallas_call(
        last_kernel,
        out_shape=jax.ShapeDtypeStruct((rhs, leaves * pts), BF16),
        in_specs=[SMEM] + [VMEM] * 13,
        out_specs=VMEM,
        scratch_shapes=[pltpu.VMEM((n, rhs, rank), F32) for n in (16, 8, 4)],
        name="last",
        compiler_params=params,
    )(d.reshape(1), far_pattern.T, transfer, coupling, basis, m0, m1, m2, m3, m4, m5, m6, g7, near)
    return product.T


def solution(mesh):
    leaf, sub = mesh.shape["leaf"], mesh.shape["sub"]
    cut = Mesh(mesh.devices.reshape(leaf // 8, 4, 2, sub), AXES)
    placed = (
        P(AXES, None),
        P(AXES, None, None),
        P(),
        P(),
        P(AXES, None, None, None),
        P(AXES, None),
        P(),
    )
    return jax.shard_map(shards, mesh=cut, in_specs=placed, out_specs=P(AXES, None), check_vma=False)
```

```python
import jax
import jax.numpy as jnp
from jax import lax
from jax.experimental import pallas as pl
from jax.experimental.pallas import tpu as pltpu
from jax.sharding import Mesh, PartitionSpec as P

AXES = ("z", "y", "c", "x")
F32 = jnp.float32
BF16 = jnp.bfloat16
NN = (((1,), (0,)), ((), ()))
NT = (((1,), (1,)), ((), ()))
VMEM = pl.BlockSpec(memory_space=pltpu.VMEM)
SMEM = pl.BlockSpec(memory_space=pltpu.SMEM)
HBM = pl.BlockSpec(memory_space=pltpu.HBM)
PARAMS = pltpu.CompilerParams(vmem_limit_bytes=40 * 1024 * 1024)


def in_hbm(array):
    return pltpu.with_memory_space_constraint(array, pltpu.HBM)


def split(a):
    high = a.astype(BF16)
    return high, (a - high.astype(F32)).astype(BF16)


def dot(a, b, dims):
    return lax.dot_general(a, b, dims, preferred_element_type=F32)


def dot3(a, b, dims):
    return dot(a[0], b[0], dims) + (dot(a[0], b[1], dims) + dot(a[1], b[0], dims))


def lift(first, second, transfer):
    return dot3(split(first), transfer[0], NN) + dot3(split(second), transfer[1], NN)


def pair_of(first, second):
    return jnp.concatenate([first, second], axis=1)


def device_index():
    z, y, c, x = (lax.axis_index(a) for a in AXES)
    return ((z * lax.axis_size("y") + y) * lax.axis_size("c") + c) * lax.axis_size("x") + x


def device_count():
    count = 1
    for a in AXES:
        count *= lax.axis_size(a)
    return count


def swap(array, mask):
    return lax.ppermute(array, AXES, [(i, i ^ mask) for i in range(device_count())])


def across(device, step, count):
    return (device + jnp.where(device & step, step, count - step)) % count


def swap_across(array, step):
    n = device_count()
    pairs = [(i, (i + (step if i & step else n - step)) % n) for i in range(n)]
    return lax.ppermute(array, AXES, pairs)


def leaf_kernel(src_in, basis_in, transfer_in, coupling_in, far_in, src, basis, coupling, far, tsplit, m0, m1, pair2, raw, sems):
    copies = [
        pltpu.make_async_copy(a, b, sems.at[i])
        for i, (a, b) in enumerate(
            ((src_in, src), (basis_in, basis), (transfer_in, raw), (coupling_in, coupling), (far_in, far))
        )
    ]
    for copy in copies:
        copy.start()
    for copy in copies[:3]:
        copy.wait()
    t = [split(raw[i]) for i in range(2)]
    for i in range(2):
        tsplit[2 * i], tsplit[2 * i + 1] = t[i]
    leaves, _, pts = basis.shape
    low = []
    for i in range(leaves):
        v = dot(src[:, i * pts : (i + 1) * pts], basis[i], NT)
        m0[i] = v
        low.append(v)
    mid = [lift(low[2 * i], low[2 * i + 1], t) for i in range(leaves // 2)]
    for i, v in enumerate(mid):
        m1[i] = v
    pair2[...] = pair_of(lift(mid[0], mid[1], t), lift(mid[2], mid[3], t))
    for copy in copies[3:]:
        copy.wait()


def transfers(tsplit):
    return [(tsplit[0], tsplit[1]), (tsplit[2], tsplit[3])]


def clusters(pairs, out):
    for i, p in enumerate(pairs):
        out[2 * i] = p[:, :64]
        out[2 * i + 1] = p[:, 64:]


def up4_kernel(copies, axis, refs):
    own, p1, p2, p3, tsplit = refs[:5]
    a, b, pair, ordered = refs[-4:]
    t = transfers(tsplit)
    here = lax.axis_index(axis)
    for i, ref in enumerate((own, p1, p2, p3)):
        ordered[here ^ i] = ref[...]
    clusters([ordered[i] for i in range(4)], a)
    low = [a[i] for i in range(8)]
    mid = [lift(low[2 * i], low[2 * i + 1], t) for i in range(4)]
    for i, v in enumerate(mid):
        b[i] = v
    top = pair_of(lift(mid[0], mid[1], t), lift(mid[2], mid[3], t))
    if copies:
        for i in range(copies):
            pair[i] = top
    else:
        pair[...] = top


def up2_kernel(axis, refs):
    own, p1, tsplit = refs[:3]
    a, pair, ordered = refs[-3:]
    t = transfers(tsplit)
    here = lax.axis_index(axis)
    for i, ref in enumerate((own, p1)):
        ordered[here ^ i] = ref[...]
    clusters([ordered[i] for i in range(2)], a)
    pair[...] = pair_of(lift(a[0], a[1], t), lift(a[2], a[3], t))


def near_kernel(pattern_in, own, core, side, cross4, cross1, blocks_in, out, held, blocks, pattern, sems, sem):
    leaves, slots, pts = blocks_in.shape[:3]
    pattern_copy = pltpu.make_async_copy(pattern_in, pattern, sem)
    pattern_copy.start()
    copies = [pltpu.make_async_copy(blocks_in.at[i], blocks.at[i], sems.at[i]) for i in range(leaves)]
    for copy in copies:
        copy.start()
    for n, ref in enumerate((own, core, side, cross4, cross1)):
        for i in range(leaves):
            held[n * leaves + i] = ref[:, i * pts : (i + 1) * pts]
    pattern_copy.wait()
    me = device_index()
    n = device_count()
    others = [me, me ^ 4, me ^ 1, across(me, 4, n)]
    for i in range(leaves):
        copies[i].wait()
        total = None
        for s in range(slots):
            j = pattern[s, i]
            device = j // leaves
            slot = jnp.int32(4)
            for k, other in enumerate(others):
                slot = jnp.where(device == other, k, slot)
            term = dot(held[slot * leaves + j % leaves], blocks[i, s], NT)
            total = term if total is None else total + term
        out[:, i * pts : (i + 1) * pts] = total


def start_of(level):
    return sum(2048 >> l for l in range(level))


def weights_of(far, level, cluster):
    row = start_of(level) + cluster
    total = far.shape[1]
    tail = total // 128 * 128
    if start_of(level) >= tail:
        chunk, base = far[:, tail:], tail
    else:
        base = row // 128 * 128
        chunk = far[:, pl.ds(pl.multiple_of(base, 128), 128)]
    lane = lax.broadcasted_iota(jnp.int32, chunk.shape, 1)
    w = jnp.sum(jnp.where(lane == row - base, chunk, 0), axis=1, keepdims=True).astype(F32)
    return [w[j : j + 1, :] for j in range(3)]


def couple(weights, sources, coupling):
    total = None
    for w, m, c in zip(weights, sources, coupling):
        term = dot3(split(m * w), c, NT)
        total = term if total is None else total + term
    return total


def local(far, c, level, cluster, values, width):
    at = cluster % width
    group = at // 4 * 4
    return couple(weights_of(far, level, cluster), [values[group + (at + j) % 4] for j in (1, 2, 3)], c)


def low_kernel(far, coupling, m0, m1, loc0, loc1):
    c = [split(coupling[i]) for i in range(3)]
    d = device_index()
    for level, values, out in ((0, m0, loc0), (1, m1, loc1)):
        count = values.shape[0]
        for i in range(count):
            w = weights_of(far, level, d * count + i)
            out[i] = couple(w, [values[i // 4 * 4 + (i + j) % 4] for j in (1, 2, 3)], c)


def low2_kernel(far, coupling, m2, behind, loc2):
    c = [split(coupling[i]) for i in range(3)]
    d = device_index()
    for i in range(2):
        loc2[i] = local(far, c, 2, d * 2 + i, m2, 8)


def mid_kernel(far, coupling, tsplit, basis, loc0, loc1, loc2, m3, m4, m5, m6, near, part, ghigh, glow):
    c = [split(coupling[i]) for i in range(3)]
    t = transfers(tsplit)
    d = device_index()
    rows = lax.broadcasted_iota(jnp.int32, (64, 64), 0)
    cols = lax.broadcasted_iota(jnp.int32, (64, 64), 1)
    chain = jnp.where(rows == cols, 1.0, 0.0).astype(F32)
    field = None
    for level, values, width in ((6, m6, 4), (5, m5, 8), (4, m4, 4), (3, m3, 4)):
        cluster = d >> (level - 3)
        child = cluster % 2
        one = (tsplit[2 * child], tsplit[2 * child + 1])
        own = local(far, c, level, cluster, values, width)
        if field is None:
            chain = dot3(split(chain), one, NT)
            field = own
        else:
            both = dot3(split(jnp.concatenate([field, chain], 0)), one, NT)
            field, chain = own + both[:64], both[64:]
    parents = [(field, chain)]
    for level, count in ((2, 2), (1, 4), (0, 8)):
        below = []
        for i in range(count):
            own = (loc0, loc1, loc2)[level][i]
            both = dot3(split(jnp.concatenate(parents[i // 2], 0)), t[i % 2], NT)
            below.append((own + both[:64], both[64:]))
        parents = below
    pts = basis.shape[2]
    for i, both in enumerate(parents):
        high, low = split(jnp.concatenate(both, 0))
        whole = dot(high, basis[i], NN) + dot(low, basis[i], NN)
        at = slice(i * pts, (i + 1) * pts)
        part[:, at] = whole[:64] + near[:, at]
        ghigh[:, at], glow[:, at] = split(whole[64:])


def last_kernel(far, coupling, tsplit, g7, part, ghigh, glow, out, m7, m8, m9):
    c = [split(coupling[i]) for i in range(3)]
    t = transfers(tsplit)
    d = device_index()
    clusters([g7[i] for i in range(8)], m7)
    for i in range(8):
        m8[i] = lift(m7[2 * i], m7[2 * i + 1], t)
    for i in range(4):
        m9[i] = lift(m8[2 * i], m8[2 * i + 1], t)
    field = local(far, c, 9, d >> 6, m9, 4)
    for level, values, width in ((8, m8, 8), (7, m7, 16)):
        cluster = d >> (level - 3)
        child = cluster % 2
        one = (tsplit[2 * child], tsplit[2 * child + 1])
        field = local(far, c, level, cluster, values, width) + dot3(split(field), one, NT)
    high, low = split(field)
    step = 256
    for at in range(0, out.shape[1], step):
        at = slice(at, at + step)
        far_part = dot(high, ghigh[:, at], NN) + (dot(high, glow[:, at], NN) + dot(low, ghigh[:, at], NN))
        out[:, at] = (far_part + part[:, at]).astype(BF16)


def shards(sources, leaf_basis, transfer, coupling, near_blocks, near_pattern, far_pattern):
    leaves, pts, rank = leaf_basis.shape
    rhs = sources.shape[1]
    points = leaves * pts
    src_in = sources.T
    basis_in = jnp.swapaxes(leaf_basis, 1, 2)
    far_in = far_pattern.T
    of = jax.ShapeDtypeStruct
    mat = lambda n: of((n, rhs, rank), F32)
    pair = of((rhs, 2 * rank), F32)

    src, basis, coup, far, tsplit, m0, m1, pair2 = pl.pallas_call(
        leaf_kernel,
        out_shape=(
            of(src_in.shape, BF16), of(basis_in.shape, BF16), of(coupling.shape, F32), of(far_in.shape, jnp.int32),
            of((4, rank, rank), BF16), mat(8), mat(4), pair,
        ),
        in_specs=[HBM] * 5, out_specs=(VMEM,) * 8,
        scratch_shapes=[pltpu.VMEM(transfer.shape, F32), pltpu.SemaphoreType.DMA((5,))],
        name="leaf", compiler_params=PARAMS,
    )(*[in_hbm(a) for a in (src_in, basis_in, transfer, coupling, far_in)])

    def up4(own, masks, axis, copies, *behind):
        got = [swap(own, m) for m in masks]
        top = of((copies,) + pair.shape, F32) if copies else pair
        return pl.pallas_call(
            lambda *refs: up4_kernel(copies, axis, refs),
            out_shape=(mat(8), mat(4), top), in_specs=[VMEM] * (5 + len(behind)), out_specs=(VMEM,) * 3,
            scratch_shapes=[pltpu.VMEM((4,) + pair.shape, F32)], name="up4", compiler_params=PARAMS,
        )(own, *got, tsplit, *behind)

    def up2(own, mask, axis, *behind):
        return pl.pallas_call(
            lambda *refs: up2_kernel(axis, refs),
            out_shape=(mat(4), pair), in_specs=[VMEM] * (3 + len(behind)), out_specs=(VMEM,) * 2,
            scratch_shapes=[pltpu.VMEM((2,) + pair.shape, F32)], name="up2", compiler_params=PARAMS,
        )(own, swap(own, mask), tsplit, *behind)

    def later(array, other):
        return lax.optimization_barrier((array, other))[0]

    loc0, loc1 = pl.pallas_call(
        low_kernel, out_shape=(mat(8), mat(4)), in_specs=[VMEM] * 4, out_specs=(VMEM,) * 2,
        name="low", compiler_params=PARAMS,
    )(far, coup, m0, m1)
    cross1 = swap_across(later(src, loc0), 1)
    m2, m3, pair4 = up4(pair2, (1, 2, 3), "x", 0, loc0)
    cross4 = swap_across(later(src, pair4), 4)
    m4, pair5 = up2(pair4, 4, "c", loc0)
    loc2 = pl.pallas_call(
        low2_kernel, out_shape=mat(2), in_specs=[VMEM] * 4, out_specs=VMEM,
        name="low2", compiler_params=PARAMS,
    )(far, coup, m2, pair5)
    src3 = later(src, loc2)
    core, side = swap(src3, 4), swap(src3, 1)

    near = pl.pallas_call(
        near_kernel,
        out_shape=of((rhs, points), F32),
        in_specs=[HBM] + [VMEM] * 5 + [HBM], out_specs=VMEM,
        scratch_shapes=[
            pltpu.VMEM((5 * leaves, rhs, pts), BF16),
            pltpu.VMEM(near_blocks.shape, BF16),
            pltpu.SMEM(near_pattern.shape[::-1], jnp.int32),
            pltpu.SemaphoreType.DMA((leaves,)),
            pltpu.SemaphoreType.DMA,
        ],
        name="near", compiler_params=PARAMS,
    )(in_hbm(near_pattern.T), src, core, side, cross4, cross1, in_hbm(near_blocks))

    m5, m6, pair7 = up4(pair5, (8, 16, 24), "y", 8, loc2, cross4, cross1)
    g7 = lax.all_to_all(pair7, "z", 0, 0, tiled=True)

    part, ghigh, glow = pl.pallas_call(
        mid_kernel,
        out_shape=(of((rhs, points), F32), of((rhs, points), BF16), of((rhs, points), BF16)),
        in_specs=[VMEM] * 12, out_specs=(VMEM,) * 3,
        name="mid", compiler_params=PARAMS,
    )(far, coup, tsplit, basis, loc0, loc1, loc2, m3, m4, m5, m6, near)

    product = pl.pallas_call(
        last_kernel,
        out_shape=of((rhs, points), BF16),
        in_specs=[VMEM] * 7, out_specs=VMEM,
        scratch_shapes=[pltpu.VMEM((n, rhs, rank), F32) for n in (16, 8, 4)],
        name="last", compiler_params=PARAMS,
    )(far, coup, tsplit, g7, part, ghigh, glow)
    return product.T


def solution(mesh):
    leaf, sub = mesh.shape["leaf"], mesh.shape["sub"]
    cut = Mesh(mesh.devices.reshape(leaf // 8, 4, 2, sub), AXES)
    placed = (
        P(AXES, None),
        P(AXES, None, None),
        P(),
        P(),
        P(AXES, None, None, None),
        P(AXES, None),
        P(),
    )
    return jax.shard_map(shards, mesh=cut, in_specs=placed, out_specs=P(AXES, None), check_vma=False)
```

```python
import jax
import jax.numpy as jnp
from jax import lax
from jax.experimental import pallas as pl
from jax.experimental.pallas import tpu as pltpu
from jax.sharding import Mesh, PartitionSpec as P

AXES = ("z", "y", "c", "x")
F32 = jnp.float32
BF16 = jnp.bfloat16
NN = (((1,), (0,)), ((), ()))
NT = (((1,), (1,)), ((), ()))
VMEM = pl.BlockSpec(memory_space=pltpu.VMEM)
SMEM = pl.BlockSpec(memory_space=pltpu.SMEM)
HBM = pl.BlockSpec(memory_space=pltpu.HBM)
PARAMS = pltpu.CompilerParams(vmem_limit_bytes=4 * 1024 * 1024)


def in_hbm(array):
    return pltpu.with_memory_space_constraint(array, pltpu.HBM)


def split(a):
    high = a.astype(BF16)
    return high, (a - high.astype(F32)).astype(BF16)


def dot(a, b, dims):
    return lax.dot_general(a, b, dims, preferred_element_type=F32)


def dot3(a, b, dims):
    return dot(a[0], b[0], dims) + (dot(a[0], b[1], dims) + dot(a[1], b[0], dims))


def lift(first, second, transfer):
    return dot3(split(first), transfer[0], NN) + dot3(split(second), transfer[1], NN)


def pair_of(first, second):
    return jnp.concatenate([first, second], axis=1)


def device_index():
    z, y, c, x = (lax.axis_index(a) for a in AXES)
    return ((z * lax.axis_size("y") + y) * lax.axis_size("c") + c) * lax.axis_size("x") + x


def device_count():
    count = 1
    for a in AXES:
        count *= lax.axis_size(a)
    return count


def swap(array, mask):
    return lax.ppermute(array, AXES, [(i, i ^ mask) for i in range(device_count())])


def across(device, step, count):
    return (device + jnp.where(device & step, step, count - step)) % count


def swap_across(array, step):
    n = device_count()
    pairs = [(i, (i + (step if i & step else n - step)) % n) for i in range(n)]
    return lax.ppermute(array, AXES, pairs)


def leaf_kernel(src_in, basis_in, transfer_in, coupling_in, far_in, src, coupling, far, tsplit, m0, m1, pair2, basis, raw, sems):
    copies = [
        pltpu.make_async_copy(a, b, sems.at[i])
        for i, (a, b) in enumerate(
            ((src_in, src), (basis_in, basis), (transfer_in, raw), (coupling_in, coupling), (far_in, far))
        )
    ]
    for copy in copies:
        copy.start()
    for copy in copies[:3]:
        copy.wait()
    t = [split(raw[i]) for i in range(2)]
    for i in range(2):
        tsplit[2 * i], tsplit[2 * i + 1] = t[i]
    leaves, _, pts = basis.shape
    low = []
    for i in range(leaves):
        v = dot(src[:, i * pts : (i + 1) * pts], basis[i], NT)
        m0[i] = v
        low.append(v)
    mid = [lift(low[2 * i], low[2 * i + 1], t) for i in range(leaves // 2)]
    for i, v in enumerate(mid):
        m1[i] = v
    pair2[...] = pair_of(lift(mid[0], mid[1], t), lift(mid[2], mid[3], t))
    for copy in copies[3:]:
        copy.wait()


def transfers(tsplit):
    return [(tsplit[0], tsplit[1]), (tsplit[2], tsplit[3])]


def clusters(pairs, out):
    for i, p in enumerate(pairs):
        out[2 * i] = p[:, :64]
        out[2 * i + 1] = p[:, 64:]


def up4_kernel(copies, axis, refs):
    own, p1, p2, p3, tsplit = refs[:5]
    ab, pair, ordered = refs[-3:]
    t = transfers(tsplit)
    here = lax.axis_index(axis)
    for i, ref in enumerate((own, p1, p2, p3)):
        ordered[here ^ i] = ref[...]
    clusters([ordered[i] for i in range(4)], ab)
    low = [ab[i] for i in range(8)]
    mid = [lift(low[2 * i], low[2 * i + 1], t) for i in range(4)]
    for i, v in enumerate(mid):
        ab[8 + i] = v
    top = pair_of(lift(mid[0], mid[1], t), lift(mid[2], mid[3], t))
    if copies:
        for i in range(copies):
            pair[i] = top
    else:
        pair[...] = top


def up2_kernel(axis, refs):
    own, p1, tsplit = refs[:3]
    a, pair, ordered = refs[-3:]
    t = transfers(tsplit)
    here = lax.axis_index(axis)
    for i, ref in enumerate((own, p1)):
        ordered[here ^ i] = ref[...]
    clusters([ordered[i] for i in range(2)], a)
    pair[...] = pair_of(lift(a[0], a[1], t), lift(a[2], a[3], t))


def start_of(level):
    return sum(2048 >> l for l in range(level))


def weights_of(far, level, cluster):
    row = start_of(level) + cluster
    total = far.shape[1]
    tail = total // 128 * 128
    if start_of(level) >= tail:
        chunk, base = far[:, tail:], tail
    else:
        base = row // 128 * 128
        chunk = far[:, pl.ds(pl.multiple_of(base, 128), 128)]
    lane = lax.broadcasted_iota(jnp.int32, chunk.shape, 1)
    w = jnp.sum(jnp.where(lane == row - base, chunk, 0), axis=1, keepdims=True).astype(F32)
    return [w[j : j + 1, :] for j in range(3)]


def couple(weights, sources, coupling):
    total = None
    for w, m, c in zip(weights, sources, coupling):
        term = dot3(split(m * w), c, NT)
        total = term if total is None else total + term
    return total


def local(far, c, level, cluster, values, width, first=0):
    at = cluster % width
    group = at // 4 * 4 + first
    return couple(weights_of(far, level, cluster), [values[group + (at + j) % 4] for j in (1, 2, 3)], c)


def low_kernel(far, coupling, m1, loc_a):
    c = [split(coupling[i]) for i in range(3)]
    d = device_index()
    for i in range(4):
        w = weights_of(far, 1, d * 4 + i)
        loc_a[i] = couple(w, [m1[(i + j) % 4] for j in (1, 2, 3)], c)


def low2_kernel(far, coupling, m0, m23, m4, behind, loc_b):
    c = [split(coupling[i]) for i in range(3)]
    d = device_index()
    for i in range(8):
        w = weights_of(far, 0, d * 8 + i)
        loc_b[4 + i] = couple(w, [m0[i // 4 * 4 + (i + j) % 4] for j in (1, 2, 3)], c)
    for i in range(2):
        loc_b[i] = local(far, c, 2, d * 2 + i, m23, 8)
    loc_b[2] = local(far, c, 3, d, m23, 4, 8)
    loc_b[3] = local(far, c, 4, d >> 1, m4, 4)


def mid_kernel(far, coupling, tsplit, loc_a, loc_b, m56, core, side, cross4, cross1,
               src_in, basis_in, pattern_in, blocks_in, part, g, held, basis, blocks, pattern, sems, own_sems, pair_sems):
    leaves, slots, pts = blocks_in.shape[:3]
    own_copies = [
        pltpu.make_async_copy(src_in.at[:, i * pts : (i + 1) * pts], held.at[i], own_sems.at[i]) for i in range(leaves)
    ]
    for copy in own_copies:
        copy.start()
    basis_copy = pltpu.make_async_copy(basis_in, basis, pair_sems.at[0])
    basis_copy.start()
    pattern_copy = pltpu.make_async_copy(pattern_in, pattern, pair_sems.at[1])
    pattern_copy.start()
    copies = [pltpu.make_async_copy(blocks_in.at[i], blocks.at[i], sems.at[i]) for i in range(leaves)]
    for copy in copies:
        copy.start()

    c = [split(coupling[i]) for i in range(3)]
    t = transfers(tsplit)
    d = device_index()
    rows = lax.broadcasted_iota(jnp.int32, (64, 64), 0)
    cols = lax.broadcasted_iota(jnp.int32, (64, 64), 1)
    chain = jnp.where(rows == cols, 1.0, 0.0).astype(F32)
    field = None
    for level, width, first in ((6, 4, 8), (5, 8, 0), (4, 0, 0), (3, 0, 0)):
        cluster = d >> (level - 3)
        child = cluster % 2
        one = (tsplit[2 * child], tsplit[2 * child + 1])
        here = local(far, c, level, cluster, m56, width, first) if width else loc_b[level - 1]
        if field is None:
            chain = dot3(split(chain), one, NT)
            field = here
        else:
            both = dot3(split(jnp.concatenate([field, chain], 0)), one, NT)
            field, chain = here + both[:64], both[64:]
    parents = [(field, chain)]
    for locs, first, count in ((loc_b, 0, 2), (loc_a, 0, 4), (loc_b, 4, 8)):
        below = []
        for i in range(count):
            both = dot3(split(jnp.concatenate(parents[i // 2], 0)), t[i % 2], NT)
            below.append((locs[first + i] + both[:64], both[64:]))
        parents = below

    for n, ref in enumerate((core, side, cross4, cross1)):
        for i in range(leaves):
            held[(n + 1) * leaves + i] = ref[:, i * pts : (i + 1) * pts]
    for copy in own_copies:
        copy.wait()
    basis_copy.wait()
    pattern_copy.wait()
    others = [d, d ^ 4, d ^ 1, across(d, 4, device_count())]
    for i, both in enumerate(parents):
        at = slice(i * pts, (i + 1) * pts)
        high, low = split(jnp.concatenate(both, 0))
        whole = dot(high, basis[i], NN) + dot(low, basis[i], NN)
        g[0, :, at], g[1, :, at] = split(whole[64:])
        copies[i].wait()
        total = whole[:64]
        for s in range(slots):
            j = pattern[s, i]
            device = j // leaves
            slot = jnp.int32(4)
            for k, other in enumerate(others):
                slot = jnp.where(device == other, k, slot)
            total = total + dot(held[slot * leaves + j % leaves], blocks[i, s], NT)
        part[:, at] = total


def last_kernel(far, coupling, tsplit, g7, part, g, out, m7, m8, m9):
    c = [split(coupling[i]) for i in range(3)]
    t = transfers(tsplit)
    d = device_index()
    clusters([g7[i] for i in range(8)], m7)
    for i in range(8):
        m8[i] = lift(m7[2 * i], m7[2 * i + 1], t)
    for i in range(4):
        m9[i] = lift(m8[2 * i], m8[2 * i + 1], t)
    field = local(far, c, 9, d >> 6, m9, 4)
    for level, values, width in ((8, m8, 8), (7, m7, 16)):
        cluster = d >> (level - 3)
        child = cluster % 2
        one = (tsplit[2 * child], tsplit[2 * child + 1])
        field = local(far, c, level, cluster, values, width) + dot3(split(field), one, NT)
    high, low = split(field)
    step = 256
    for at in range(0, out.shape[1], step):
        at = slice(at, at + step)
        far_part = dot(high, g[0, :, at], NN) + (dot(high, g[1, :, at], NN) + dot(low, g[0, :, at], NN))
        out[:, at] = (far_part + part[:, at]).astype(BF16)


def shards(sources, leaf_basis, transfer, coupling, near_blocks, near_pattern, far_pattern):
    leaves, pts, rank = leaf_basis.shape
    rhs = sources.shape[1]
    points = leaves * pts
    src_in = sources.T
    basis_in = jnp.swapaxes(leaf_basis, 1, 2)
    far_in = far_pattern.T
    of = jax.ShapeDtypeStruct
    mat = lambda n: of((n, rhs, rank), F32)
    pair = of((rhs, 2 * rank), F32)

    src, coup, far, tsplit, m0, m1, pair2 = pl.pallas_call(
        leaf_kernel,
        out_shape=(
            of(src_in.shape, BF16), of(coupling.shape, F32), of(far_in.shape, jnp.int32),
            of((4, rank, rank), BF16), mat(8), mat(4), pair,
        ),
        in_specs=[HBM] * 5, out_specs=(VMEM,) * 7,
        scratch_shapes=[pltpu.VMEM(basis_in.shape, BF16), pltpu.VMEM(transfer.shape, F32), pltpu.SemaphoreType.DMA((5,))],
        name="leaf", compiler_params=PARAMS,
    )(*[in_hbm(a) for a in (src_in, basis_in, transfer, coupling, far_in)])

    def up4(own, masks, axis, copies, *behind):
        got = [swap(own, m) for m in masks]
        top = of((copies,) + pair.shape, F32) if copies else pair
        return pl.pallas_call(
            lambda *refs: up4_kernel(copies, axis, refs),
            out_shape=(mat(12), top), in_specs=[VMEM] * (5 + len(behind)), out_specs=(VMEM,) * 2,
            scratch_shapes=[pltpu.VMEM((4,) + pair.shape, F32)], name="up4", compiler_params=PARAMS,
        )(own, *got, tsplit, *behind)

    def up2(own, mask, axis, *behind):
        return pl.pallas_call(
            lambda *refs: up2_kernel(axis, refs),
            out_shape=(mat(4), pair), in_specs=[VMEM] * (3 + len(behind)), out_specs=(VMEM,) * 2,
            scratch_shapes=[pltpu.VMEM((2,) + pair.shape, F32)], name="up2", compiler_params=PARAMS,
        )(own, swap(own, mask), tsplit, *behind)

    def later(array, other):
        return lax.optimization_barrier((array, other))[0]

    loc_a = pl.pallas_call(
        low_kernel, out_shape=mat(4), in_specs=[VMEM] * 3, out_specs=VMEM,
        name="low", compiler_params=PARAMS,
    )(far, coup, m1)
    s2 = later(src, loc_a)
    core, cross4 = swap(s2, 4), swap_across(s2, 4)
    m23, pair4 = up4(pair2, (1, 2, 3), "x", 0, loc_a)
    s3 = later(src, pair4)
    side, cross1 = swap(s3, 1), swap_across(s3, 1)
    m4, pair5 = up2(pair4, 4, "c", cross4, core)
    loc_b = pl.pallas_call(
        low2_kernel, out_shape=mat(12), in_specs=[VMEM] * 6, out_specs=VMEM,
        name="low2", compiler_params=PARAMS,
    )(far, coup, m0, m23, m4, pair5)

    m56, pair7 = up4(pair5, (8, 16, 24), "y", 8, loc_b, cross1, side)
    g7 = lax.all_to_all(pair7, "z", 0, 0, tiled=True)

    part, g = pl.pallas_call(
        mid_kernel,
        out_shape=(of((rhs, points), F32), of((2, rhs, points), BF16)),
        in_specs=[VMEM] * 10 + [HBM] * 4, out_specs=(VMEM,) * 2,
        scratch_shapes=[
            pltpu.VMEM((5 * leaves, rhs, pts), BF16),
            pltpu.VMEM(basis_in.shape, BF16),
            pltpu.VMEM(near_blocks.shape, BF16),
            pltpu.SMEM(near_pattern.shape[::-1], jnp.int32),
            pltpu.SemaphoreType.DMA((leaves,)),
            pltpu.SemaphoreType.DMA((leaves,)),
            pltpu.SemaphoreType.DMA((2,)),
        ],
        name="mid", compiler_params=pltpu.CompilerParams(vmem_limit_bytes=8 * 1024 * 1024),
    )(far, coup, tsplit, loc_a, loc_b, m56, core, side, cross4, cross1,
      in_hbm(src_in), in_hbm(basis_in), in_hbm(near_pattern.T), in_hbm(near_blocks))

    product = pl.pallas_call(
        last_kernel,
        out_shape=of((rhs, points), BF16),
        in_specs=[VMEM] * 6, out_specs=VMEM,
        scratch_shapes=[pltpu.VMEM((n, rhs, rank), F32) for n in (16, 8, 4)],
        name="last", compiler_params=PARAMS,
    )(far, coup, tsplit, g7, part, g)
    return product.T


def solution(mesh):
    leaf, sub = mesh.shape["leaf"], mesh.shape["sub"]
    cut = Mesh(mesh.devices.reshape(leaf // 8, 4, 2, sub), AXES)
    placed = (
        P(AXES, None),
        P(AXES, None, None),
        P(),
        P(),
        P(AXES, None, None, None),
        P(AXES, None),
        P(),
    )
    return jax.shard_map(shards, mesh=cut, in_specs=placed, out_specs=P(AXES, None), check_vma=False)
```

```python
import jax
import jax.numpy as jnp
from jax import lax
from jax.experimental import pallas as pl
from jax.experimental.pallas import tpu as pltpu
from jax.sharding import Mesh, PartitionSpec as P

AXES = ("z", "y", "c", "x")
F32 = jnp.float32
BF16 = jnp.bfloat16
NN = (((1,), (0,)), ((), ()))
NT = (((1,), (1,)), ((), ()))
VMEM = pl.BlockSpec(memory_space=pltpu.VMEM)
SMEM = pl.BlockSpec(memory_space=pltpu.SMEM)
HBM = pl.BlockSpec(memory_space=pltpu.HBM)
PARAMS = pltpu.CompilerParams(vmem_limit_bytes=4 * 1024 * 1024)


def in_hbm(array):
    return pltpu.with_memory_space_constraint(array, pltpu.HBM)


def split(a):
    high = a.astype(BF16)
    return high, (a - high.astype(F32)).astype(BF16)


def dot(a, b, dims):
    return lax.dot_general(a, b, dims, preferred_element_type=F32)


def dot3(a, b, dims):
    return dot(a[0], b[0], dims) + (dot(a[0], b[1], dims) + dot(a[1], b[0], dims))


def lift(first, second, transfer):
    return dot3(split(first), transfer[0], NN) + dot3(split(second), transfer[1], NN)


def pair_of(first, second):
    return jnp.concatenate([first, second], axis=1)


def device_index():
    z, y, c, x = (lax.axis_index(a) for a in AXES)
    return ((z * lax.axis_size("y") + y) * lax.axis_size("c") + c) * lax.axis_size("x") + x


def device_count():
    count = 1
    for a in AXES:
        count *= lax.axis_size(a)
    return count


def swap(array, mask):
    return lax.ppermute(array, AXES, [(i, i ^ mask) for i in range(device_count())])


def across(device, step, count):
    return (device + jnp.where(device & step, step, count - step)) % count


def swap_across(array, step):
    n = device_count()
    pairs = [(i, (i + (step if i & step else n - step)) % n) for i in range(n)]
    return lax.ppermute(array, AXES, pairs)


def shift(array):
    n, span = device_count(), lax.axis_size("x")
    step = lambda i: -1 if i // span % 2 else 1
    return lax.ppermute(array, AXES, [(i, i // span * span + (i + step(i)) % span) for i in range(n)])


def leaf_kernel(src_in, basis_in, transfer_in, coupling_in, far_in, src, coupling, far, tsplit, m0, m1, pair2, basis, raw, sems):
    copies = [
        pltpu.make_async_copy(a, b, sems.at[i])
        for i, (a, b) in enumerate(
            ((src_in, src), (basis_in, basis), (transfer_in, raw), (coupling_in, coupling), (far_in, far))
        )
    ]
    for copy in copies:
        copy.start()
    for copy in copies[:3]:
        copy.wait()
    t = [split(raw[i]) for i in range(2)]
    for i in range(2):
        tsplit[2 * i], tsplit[2 * i + 1] = t[i]
    leaves, _, pts = basis.shape
    low = []
    for i in range(leaves):
        v = dot(src[:, i * pts : (i + 1) * pts], basis[i], NT)
        m0[i] = v
        low.append(v)
    mid = [lift(low[2 * i], low[2 * i + 1], t) for i in range(leaves // 2)]
    for i, v in enumerate(mid):
        m1[i] = v
    pair2[...] = pair_of(lift(mid[0], mid[1], t), lift(mid[2], mid[3], t))
    for copy in copies[3:]:
        copy.wait()


def transfers(tsplit):
    return [(tsplit[0], tsplit[1]), (tsplit[2], tsplit[3])]


def clusters(pairs, out):
    for i, p in enumerate(pairs):
        out[2 * i] = p[:, :64]
        out[2 * i + 1] = p[:, 64:]


def up4_kernel(copies, axis, refs):
    own, p1, p2, p3, tsplit = refs[:5]
    ab, pair, ordered = refs[-3:]
    t = transfers(tsplit)
    here = lax.axis_index(axis)
    for i, ref in enumerate((own, p1, p2, p3)):
        ordered[here ^ i] = ref[...]
    clusters([ordered[i] for i in range(4)], ab)
    low = [ab[i] for i in range(8)]
    mid = [lift(low[2 * i], low[2 * i + 1], t) for i in range(4)]
    for i, v in enumerate(mid):
        ab[8 + i] = v
    top = pair_of(lift(mid[0], mid[1], t), lift(mid[2], mid[3], t))
    if copies:
        for i in range(copies):
            pair[i] = top
    else:
        pair[...] = top


def up2_kernel(axis, refs):
    own, p1, tsplit, src, core, cross4 = refs[:6]
    a, pair, both, ordered = refs[-4:]
    t = transfers(tsplit)
    here = lax.axis_index(axis)
    for i, ref in enumerate((own, p1)):
        ordered[here ^ i] = ref[...]
    clusters([ordered[i] for i in range(2)], a)
    pair[...] = pair_of(lift(a[0], a[1], t), lift(a[2], a[3], t))
    c, x = lax.axis_index("c"), lax.axis_index("x")
    end = x == jnp.where(c == 0, lax.axis_size("x") - 1, 0)

    @pl.when(end)
    def _():
        both[0] = cross4[...]
        both[1] = src[...]

    @pl.when(jnp.logical_not(end))
    def _():
        both[0] = src[...]
        both[1] = core[...]


def start_of(level):
    return sum(2048 >> l for l in range(level))


def weights_of(far, level, cluster):
    row = start_of(level) + cluster
    total = far.shape[1]
    tail = total // 128 * 128
    if start_of(level) >= tail:
        chunk, base = far[:, tail:], tail
    else:
        base = row // 128 * 128
        chunk = far[:, pl.ds(pl.multiple_of(base, 128), 128)]
    lane = lax.broadcasted_iota(jnp.int32, chunk.shape, 1)
    w = jnp.sum(jnp.where(lane == row - base, chunk, 0), axis=1, keepdims=True).astype(F32)
    return [w[j : j + 1, :] for j in range(3)]


def couple(weights, sources, coupling):
    total = None
    for w, m, c in zip(weights, sources, coupling):
        term = dot3(split(m * w), c, NT)
        total = term if total is None else total + term
    return total


def local(far, c, level, cluster, values, width, first=0):
    at = cluster % width
    group = at // 4 * 4 + first
    return couple(weights_of(far, level, cluster), [values[group + (at + j) % 4] for j in (1, 2, 3)], c)


def low_kernel(far, coupling, m1, loc_a):
    c = [split(coupling[i]) for i in range(3)]
    d = device_index()
    for i in range(4):
        w = weights_of(far, 1, d * 4 + i)
        loc_a[i] = couple(w, [m1[(i + j) % 4] for j in (1, 2, 3)], c)


def low2_kernel(far, coupling, m0, m23, m4, behind, loc_b):
    c = [split(coupling[i]) for i in range(3)]
    d = device_index()
    for i in range(8):
        w = weights_of(far, 0, d * 8 + i)
        loc_b[4 + i] = couple(w, [m0[i // 4 * 4 + (i + j) % 4] for j in (1, 2, 3)], c)
    for i in range(2):
        loc_b[i] = local(far, c, 2, d * 2 + i, m23, 8)
    loc_b[2] = local(far, c, 3, d, m23, 4, 8)
    loc_b[3] = local(far, c, 4, d >> 1, m4, 4)


def mid_kernel(far, coupling, tsplit, loc_a, loc_b, m56, core, cross4, shifted, other,
               src_in, basis_in, pattern_in, blocks_in, part, g, held, own, basis, blocks, pattern, sems, pair_sems):
    leaves, slots, pts = blocks_in.shape[:3]
    own_copy = pltpu.make_async_copy(src_in, own, pair_sems.at[2])
    own_copy.start()
    basis_copy = pltpu.make_async_copy(basis_in, basis, pair_sems.at[0])
    basis_copy.start()
    pattern_copy = pltpu.make_async_copy(pattern_in, pattern, pair_sems.at[1])
    pattern_copy.start()
    copies = [pltpu.make_async_copy(blocks_in.at[i], blocks.at[i], sems.at[i]) for i in range(leaves)]
    for copy in copies:
        copy.start()

    c = [split(coupling[i]) for i in range(3)]
    t = transfers(tsplit)
    d = device_index()
    rows = lax.broadcasted_iota(jnp.int32, (64, 64), 0)
    cols = lax.broadcasted_iota(jnp.int32, (64, 64), 1)
    chain = jnp.where(rows == cols, 1.0, 0.0).astype(F32)
    field = None
    for level, width, first in ((6, 4, 8), (5, 8, 0), (4, 0, 0), (3, 0, 0)):
        cluster = d >> (level - 3)
        child = cluster % 2
        one = (tsplit[2 * child], tsplit[2 * child + 1])
        here = local(far, c, level, cluster, m56, width, first) if width else loc_b[level - 1]
        if field is None:
            chain = dot3(split(chain), one, NT)
            field = here
        else:
            both = dot3(split(jnp.concatenate([field, chain], 0)), one, NT)
            field, chain = here + both[:64], both[64:]
    parents = [(field, chain)]
    for locs, first, count in ((loc_b, 0, 2), (loc_a, 0, 4), (loc_b, 4, 8)):
        below = []
        for i in range(count):
            both = dot3(split(jnp.concatenate(parents[i // 2], 0)), t[i % 2], NT)
            below.append((locs[first + i] + both[:64], both[64:]))
        parents = below

    for n, ref in enumerate((core, cross4, shifted.at[0], other)):
        for i in range(leaves):
            held[(n + 1) * leaves + i] = ref[:, i * pts : (i + 1) * pts]
    own_copy.wait()
    for i in range(leaves):
        held[i] = own[:, i * pts : (i + 1) * pts]
    basis_copy.wait()
    pattern_copy.wait()
    others = [d, d ^ 4, across(d, 4, device_count()), d + jnp.where(lax.axis_index("c") == 0, -1, 1)]
    for i, both in enumerate(parents):
        at = slice(i * pts, (i + 1) * pts)
        high, low = split(jnp.concatenate(both, 0))
        whole = dot(high, basis[i], NN) + dot(low, basis[i], NN)
        g[0, :, at], g[1, :, at] = split(whole[64:])
        copies[i].wait()
        total = whole[:64]
        for s in range(slots):
            j = pattern[s, i]
            device = j // leaves
            slot = jnp.int32(4)
            for k, other in enumerate(others):
                slot = jnp.where(device == other, k, slot)
            total = total + dot(held[slot * leaves + j % leaves], blocks[i, s], NT)
        part[:, at] = total


def last_kernel(far, coupling, tsplit, g7, part, g, out, m7, m8, m9):
    c = [split(coupling[i]) for i in range(3)]
    t = transfers(tsplit)
    d = device_index()
    clusters([g7[i] for i in range(8)], m7)
    for i in range(8):
        m8[i] = lift(m7[2 * i], m7[2 * i + 1], t)
    for i in range(4):
        m9[i] = lift(m8[2 * i], m8[2 * i + 1], t)
    field = local(far, c, 9, d >> 6, m9, 4)
    for level, values, width in ((8, m8, 8), (7, m7, 16)):
        cluster = d >> (level - 3)
        child = cluster % 2
        one = (tsplit[2 * child], tsplit[2 * child + 1])
        field = local(far, c, level, cluster, values, width) + dot3(split(field), one, NT)
    high, low = split(field)
    step = 256
    for at in range(0, out.shape[1], step):
        at = slice(at, at + step)
        far_part = dot(high, g[0, :, at], NN) + (dot(high, g[1, :, at], NN) + dot(low, g[0, :, at], NN))
        out[:, at] = (far_part + part[:, at]).astype(BF16)


def shards(sources, leaf_basis, transfer, coupling, near_blocks, near_pattern, far_pattern):
    leaves, pts, rank = leaf_basis.shape
    rhs = sources.shape[1]
    points = leaves * pts
    src_in = sources.T
    basis_in = jnp.swapaxes(leaf_basis, 1, 2)
    far_in = far_pattern.T
    of = jax.ShapeDtypeStruct
    mat = lambda n: of((n, rhs, rank), F32)
    pair = of((rhs, 2 * rank), F32)

    src, coup, far, tsplit, m0, m1, pair2 = pl.pallas_call(
        leaf_kernel,
        out_shape=(
            of(src_in.shape, BF16), of(coupling.shape, F32), of(far_in.shape, jnp.int32),
            of((4, rank, rank), BF16), mat(8), mat(4), pair,
        ),
        in_specs=[HBM] * 5, out_specs=(VMEM,) * 7,
        scratch_shapes=[pltpu.VMEM(basis_in.shape, BF16), pltpu.VMEM(transfer.shape, F32), pltpu.SemaphoreType.DMA((5,))],
        name="leaf", compiler_params=PARAMS,
    )(*[in_hbm(a) for a in (src_in, basis_in, transfer, coupling, far_in)])

    def up4(own, masks, axis, copies, *behind):
        got = [swap(own, m) for m in masks]
        top = of((copies,) + pair.shape, F32) if copies else pair
        return pl.pallas_call(
            lambda *refs: up4_kernel(copies, axis, refs),
            out_shape=(mat(12), top), in_specs=[VMEM] * (5 + len(behind)), out_specs=(VMEM,) * 2,
            scratch_shapes=[pltpu.VMEM((4,) + pair.shape, F32)], name="up4", compiler_params=PARAMS,
        )(own, *got, tsplit, *behind)

    def up2(own, mask, axis, *sources):
        return pl.pallas_call(
            lambda *refs: up2_kernel(axis, refs),
            out_shape=(mat(4), pair, of((2,) + src_in.shape, BF16)), in_specs=[VMEM] * 6, out_specs=(VMEM,) * 3,
            scratch_shapes=[pltpu.VMEM((2,) + pair.shape, F32)], name="up2", compiler_params=PARAMS,
        )(own, swap(own, mask), tsplit, *sources)

    loc_a = pl.pallas_call(
        low_kernel, out_shape=mat(4), in_specs=[VMEM] * 3, out_specs=VMEM,
        name="low", compiler_params=PARAMS,
    )(far, coup, m1)
    core, cross4 = swap(src, 4), swap_across(src, 4)
    m23, pair4 = up4(pair2, (1, 2, 3), "x", 0, loc_a)
    m4, pair5, both = up2(pair4, 4, "c", src, core, cross4)
    loc_b = pl.pallas_call(
        low2_kernel, out_shape=mat(12), in_specs=[VMEM] * 6, out_specs=VMEM,
        name="low2", compiler_params=PARAMS,
    )(far, coup, m0, m23, m4, pair5)

    shifted = shift(both)
    m56, pair7 = up4(pair5, (8, 16, 24), "y", 8, loc_b)
    g7 = lax.all_to_all(pair7, "z", 0, 0, tiled=True)
    other = swap(shifted[1], 4)

    part, g = pl.pallas_call(
        mid_kernel,
        out_shape=(of((rhs, points), F32), of((2, rhs, points), BF16)),
        in_specs=[VMEM] * 10 + [HBM] * 4, out_specs=(VMEM,) * 2,
        scratch_shapes=[
            pltpu.VMEM((5 * leaves, rhs, pts), BF16),
            pltpu.VMEM(src_in.shape, BF16),
            pltpu.VMEM(basis_in.shape, BF16),
            pltpu.VMEM(near_blocks.shape, BF16),
            pltpu.SMEM(near_pattern.shape[::-1], jnp.int32),
            pltpu.SemaphoreType.DMA((leaves,)),
            pltpu.SemaphoreType.DMA((3,)),
        ],
        name="mid", compiler_params=pltpu.CompilerParams(vmem_limit_bytes=8 * 1024 * 1024),
    )(far, coup, tsplit, loc_a, loc_b, m56, core, cross4, shifted, other,
      in_hbm(src_in), in_hbm(basis_in), in_hbm(near_pattern.T), in_hbm(near_blocks))

    product = pl.pallas_call(
        last_kernel,
        out_shape=of((rhs, points), BF16),
        in_specs=[VMEM] * 6, out_specs=VMEM,
        scratch_shapes=[pltpu.VMEM((n, rhs, rank), F32) for n in (16, 8, 4)],
        name="last", compiler_params=PARAMS,
    )(far, coup, tsplit, g7, part, g)
    return product.T


def solution(mesh):
    leaf, sub = mesh.shape["leaf"], mesh.shape["sub"]
    cut = Mesh(mesh.devices.reshape(leaf // 8, 4, 2, sub), AXES)
    placed = (
        P(AXES, None),
        P(AXES, None, None),
        P(),
        P(),
        P(AXES, None, None, None),
        P(AXES, None),
        P(),
    )
    return jax.shard_map(shards, mesh=cut, in_specs=placed, out_specs=P(AXES, None), check_vma=False)
```

```python
import jax
import jax.numpy as jnp
from jax import lax
from jax.experimental import pallas as pl
from jax.experimental.pallas import tpu as pltpu
from jax.sharding import Mesh, PartitionSpec as P

AXES = ("z", "y", "c", "x")
F32 = jnp.float32
BF16 = jnp.bfloat16
NN = (((1,), (0,)), ((), ()))
NT = (((1,), (1,)), ((), ()))
VMEM = pl.BlockSpec(memory_space=pltpu.VMEM)
SMEM = pl.BlockSpec(memory_space=pltpu.SMEM)
HBM = pl.BlockSpec(memory_space=pltpu.HBM)
ORDER = (2, 1, 3)
PARAMS = pltpu.CompilerParams(vmem_limit_bytes=4 * 1024 * 1024)


def in_hbm(array):
    return pltpu.with_memory_space_constraint(array, pltpu.HBM)


def split(a):
    high = a.astype(BF16)
    return high, (a - high.astype(F32)).astype(BF16)


def dot(a, b, dims):
    return lax.dot_general(a, b, dims, preferred_element_type=F32)


def dot3(a, b, dims):
    return dot(a[0], b[0], dims) + (dot(a[0], b[1], dims) + dot(a[1], b[0], dims))


def lift(pairs, tsplit):
    return dot3(split(pairs), (tsplit[0], tsplit[1]), NN)


def child_transfer(tsplit, child):
    at = pl.ds(pl.multiple_of(child * 64, 64), 64)
    return tsplit[0, at], tsplit[1, at]


def paired(values):
    whole = [values[i * 64 : (i + 1) * 64] for i in range(values.shape[0] // 64)]
    return jnp.concatenate([pair_of(whole[i], whole[i + 1]) for i in range(0, len(whole), 2)], axis=0)


def pair_of(first, second):
    return jnp.concatenate([first, second], axis=1)


def device_index():
    z, y, c, x = (lax.axis_index(a) for a in AXES)
    return ((z * lax.axis_size("y") + y) * lax.axis_size("c") + c) * lax.axis_size("x") + x


def device_count():
    count = 1
    for a in AXES:
        count *= lax.axis_size(a)
    return count


def swap(array, mask):
    return lax.ppermute(array, AXES, [(i, i ^ mask) for i in range(device_count())])


def across(device, step, count):
    return (device + jnp.where(device & step, step, count - step)) % count


def swap_across(array, step):
    n = device_count()
    pairs = [(i, (i + (step if i & step else n - step)) % n) for i in range(n)]
    return lax.ppermute(array, AXES, pairs)


def shift(array):
    n, span = device_count(), lax.axis_size("x")
    step = lambda i: -1 if i // span % 2 else 1
    return lax.ppermute(array, AXES, [(i, i // span * span + (i + step(i)) % span) for i in range(n)])


def leaf_kernel(src_in, basis_in, transfer_in, coupling_in, far_in, src, coupling, far, tsplit, m0, m1, pair2, basis, raw, sems):
    copies = [
        pltpu.make_async_copy(a, b, sems.at[i])
        for i, (a, b) in enumerate(
            ((src_in, src), (basis_in, basis), (transfer_in, raw), (coupling_in, coupling), (far_in, far))
        )
    ]
    for copy in copies:
        copy.start()
    for copy in copies[:3]:
        copy.wait()
    for i in range(2):
        tsplit[0, i * 64 : (i + 1) * 64], tsplit[1, i * 64 : (i + 1) * 64] = split(raw[i])
    leaves, _, pts = basis.shape
    low = []
    for i in range(leaves):
        v = dot(src[:, i * pts : (i + 1) * pts], basis[i], NT)
        m0[i] = v
        low.append(v)
    mid = lift(paired(jnp.concatenate(low, axis=0)), tsplit)
    for i in range(leaves // 2):
        m1[i] = mid[i * 64 : (i + 1) * 64]
    pair2[...] = paired(lift(paired(mid), tsplit))
    for copy in copies[3:]:
        copy.wait()


def clusters(pairs, out):
    for i, p in enumerate(pairs):
        out[2 * i] = p[:, :64]
        out[2 * i + 1] = p[:, 64:]


def up4_kernel(copies, axis, refs):
    own, p1, p2, p3, tsplit = refs[:5]
    ab, pair, ordered = refs[-3:]
    here = lax.axis_index(axis)
    for i, ref in zip((0,) + ORDER, (own, p1, p2, p3)):
        ordered[here ^ i] = ref[...]
    clusters([ordered[i] for i in range(4)], ab)
    mid = lift(jnp.concatenate([ordered[i] for i in range(4)], axis=0), tsplit)
    for i in range(4):
        ab[8 + i] = mid[i * 64 : (i + 1) * 64]
    top = paired(lift(paired(mid), tsplit))
    if copies:
        for i in range(copies):
            pair[i] = top
    else:
        pair[...] = top


def up2_kernel(axis, refs):
    own, p1, tsplit, src, cross4, core = refs[:6]
    a, pair, both, ordered = refs[-4:]
    here = lax.axis_index(axis)
    for i, ref in enumerate((own, p1)):
        ordered[here ^ i] = ref[...]
    clusters([ordered[i] for i in range(2)], a)
    pair[...] = paired(lift(jnp.concatenate([ordered[i] for i in range(2)], axis=0), tsplit))
    c, x = lax.axis_index("c"), lax.axis_index("x")
    end = x == jnp.where(c == 0, lax.axis_size("x") - 1, 0)

    @pl.when(end)
    def _():
        both[0] = cross4[...]
        both[1] = src[...]

    @pl.when(jnp.logical_not(end))
    def _():
        both[0] = src[...]
        both[1] = core[...]


def start_of(level):
    return sum(2048 >> l for l in range(level))


def weights_of(far, level, cluster):
    row = start_of(level) + cluster
    total = far.shape[1]
    tail = total // 128 * 128
    if start_of(level) >= tail:
        chunk, base = far[:, tail:], tail
    else:
        base = row // 128 * 128
        chunk = far[:, pl.ds(pl.multiple_of(base, 128), 128)]
    lane = lax.broadcasted_iota(jnp.int32, chunk.shape, 1)
    w = jnp.sum(jnp.where(lane == row - base, chunk, 0), axis=1, keepdims=True).astype(F32)
    return [w[j : j + 1, :] for j in range(3)]


def couple(weights, sources, coupling):
    total = None
    for w, m, c in zip(weights, sources, coupling):
        term = dot3(split(m * w), c, NT)
        total = term if total is None else total + term
    return total


def local(far, c, level, cluster, values, width, first=0):
    at = cluster % width
    group = at // 4 * 4 + first
    return couple(weights_of(far, level, cluster), [values[group + (at + j) % 4] for j in (1, 2, 3)], c)


def low_kernel(far, coupling, tsplit, m1, loc_a, top, d7, d8, d9):
    c = [split(coupling[i]) for i in range(3)]
    d = device_index()
    for i in range(4):
        w = weights_of(far, 1, d * 4 + i)
        loc_a[i] = couple(w, [m1[(i + j) % 4] for j in (1, 2, 3)], c)

    at7, at8, at9 = d >> 4, d >> 5, d >> 6
    turned = jnp.concatenate([coupling[i].T for i in range(3)], axis=0)
    below8 = child_transfer(tsplit, at8 % 2)
    below7 = child_transfer(tsplit, at7 % 2)
    from8 = dot3(split(turned), below7, NT)
    from9 = dot3(split(dot3(split(turned), below8, NT)), below7, NT)
    for held, values, level, at in ((d7, turned, 7, at7), (d8, from8, 8, at8), (d9, from9, 9, at9)):
        w = weights_of(far, level, at)
        held[0] = jnp.zeros((64, 64), F32)
        for j in (1, 2, 3):
            held[j] = w[j - 1] * values[(j - 1) * 64 : j * 64]
    lifts = (tsplit[0], tsplit[1])
    whole = jnp.concatenate([d9[(p - at9) & 3] for p in range(4)], axis=1)
    for count, held, at in ((8, d8, at8), (16, d7, at7)):
        both = dot3(lifts, split(whole), NN)
        parts = []
        for p in range(count):
            own = held[(p - at) & 3] * jnp.where(p >> 2 == at >> 2, 1.0, 0.0)
            half, column = p % 2 * 64, p // 2 * 64
            parts.append(both[half : half + 64, column : column + 64] + own)
        whole = jnp.concatenate(parts, axis=1) if count == 8 else jnp.concatenate(parts, axis=0)
    top[0], top[1] = split(whole)


def low2_kernel(far, coupling, m0, m23, m4, behind, loc_b):
    c = [split(coupling[i]) for i in range(3)]
    d = device_index()
    for i in range(8):
        w = weights_of(far, 0, d * 8 + i)
        loc_b[4 + i] = couple(w, [m0[i // 4 * 4 + (i + j) % 4] for j in (1, 2, 3)], c)
    for i in range(2):
        loc_b[i] = local(far, c, 2, d * 2 + i, m23, 8)
    loc_b[2] = local(far, c, 3, d, m23, 4, 8)
    loc_b[3] = local(far, c, 4, d >> 1, m4, 4)


def mid_kernel(far, coupling, tsplit, loc_a, loc_b, m56, basis_in, blocks_in, part, g, blocks, basis, sems):
    basis_copy = pltpu.make_async_copy(basis_in, basis, sems.at[0])
    basis_copy.start()
    blocks_copy = pltpu.make_async_copy(blocks_in, blocks, sems.at[1])
    blocks_copy.start()
    c = [split(coupling[i]) for i in range(3)]
    d = device_index()
    rows = lax.broadcasted_iota(jnp.int32, (64, 64), 0)
    cols = lax.broadcasted_iota(jnp.int32, (64, 64), 1)
    chain = jnp.where(rows == cols, 1.0, 0.0).astype(F32)
    zero = jnp.zeros((64, 64), F32)
    state = jnp.concatenate([zero, chain], 0)
    for level, width, first in ((6, 4, 8), (5, 8, 0), (4, 0, 0), (3, 0, 0)):
        cluster = d >> (level - 3)
        here = local(far, c, level, cluster, m56, width, first) if width else loc_b[level - 1]
        state = dot3(split(state), child_transfer(tsplit, cluster % 2), NT) + jnp.concatenate([here, zero], 0)
    for locs, first, count in ((loc_b, 0, 2), (loc_a, 0, 4), (loc_b, 4, 8)):
        parts = split(state)
        sides = [dot3(parts, (tsplit[0, k * 64 : (k + 1) * 64], tsplit[1, k * 64 : (k + 1) * 64]), NT) for k in (0, 1)]
        below = []
        for i in range(count):
            at = i // 2 * 128
            below.append(sides[i % 2][at : at + 64] + locs[first + i])
            below.append(sides[i % 2][at + 64 : at + 128])
        state = jnp.concatenate(below, 0)
    basis_copy.wait()
    leaves, _, pts = basis.shape
    high, low = split(state)
    for i in range(leaves):
        rows_at = slice(i * 128, (i + 1) * 128)
        at = slice(i * pts, (i + 1) * pts)
        whole = dot(high[rows_at], basis[i], NN) + dot(low[rows_at], basis[i], NN)
        part[:, at] = whole[:64]
        g[0, :, at], g[1, :, at] = split(whole[64:])
    blocks_copy.wait()


def near_kernel(far_part, core, cross4, shifted, other, blocks, src_in, pattern_in, part, held, own, pattern, sems):
    leaves, slots, pts = blocks.shape[:3]
    own_copy = pltpu.make_async_copy(src_in, own, sems.at[0])
    own_copy.start()
    pattern_copy = pltpu.make_async_copy(pattern_in, pattern, sems.at[1])
    pattern_copy.start()
    for n, ref in enumerate((core, cross4, shifted.at[0], other)):
        for i in range(leaves):
            held[(n + 1) * leaves + i] = ref[:, i * pts : (i + 1) * pts]
    own_copy.wait()
    for i in range(leaves):
        held[i] = own[:, i * pts : (i + 1) * pts]
    pattern_copy.wait()
    d = device_index()
    others = [d, d ^ 4, across(d, 4, device_count()), d + jnp.where(lax.axis_index("c") == 0, -1, 1)]
    for i in range(leaves):
        at = slice(i * pts, (i + 1) * pts)
        total = far_part[:, at]
        for s in range(slots):
            j = pattern[s, i]
            device = j // leaves
            slot = jnp.int32(4)
            for k, other_device in enumerate(others):
                slot = jnp.where(device == other_device, k, slot)
            total = total + dot(held[slot * leaves + j % leaves], blocks[i, s], NT)
        part[:, at] = total


def last_kernel(top, g7, part, g, out):
    moments = jnp.concatenate([g7[i] for i in range(8)], axis=1)
    field = dot3(split(moments), (top[0], top[1]), NN)
    high, low = split(field)
    both = jnp.concatenate([high, low], 0)
    step = 256
    for at in range(0, out.shape[1], step):
        at = slice(at, at + step)
        first = dot(both, g[0, :, at], NN)
        far_part = first[:64] + (first[64:] + dot(high, g[1, :, at], NN))
        out[:, at] = (far_part + part[:, at]).astype(BF16)


def shards(sources, leaf_basis, transfer, coupling, near_blocks, near_pattern, far_pattern):
    leaves, pts, rank = leaf_basis.shape
    rhs = sources.shape[1]
    points = leaves * pts
    src_in = sources.T
    basis_in = jnp.swapaxes(leaf_basis, 1, 2)
    far_in = far_pattern.T
    of = jax.ShapeDtypeStruct
    mat = lambda n: of((n, rhs, rank), F32)
    pair = of((rhs, 2 * rank), F32)

    src, coup, far, tsplit, m0, m1, pair2 = pl.pallas_call(
        leaf_kernel,
        out_shape=(
            of(src_in.shape, BF16), of(coupling.shape, F32), of(far_in.shape, jnp.int32),
            of((2, 2 * rank, rank), BF16), mat(8), mat(4), pair,
        ),
        in_specs=[HBM] * 5, out_specs=(VMEM,) * 7,
        scratch_shapes=[pltpu.VMEM(basis_in.shape, BF16), pltpu.VMEM(transfer.shape, F32), pltpu.SemaphoreType.DMA((5,))],
        name="leaf", compiler_params=PARAMS,
    )(*[in_hbm(a) for a in (src_in, basis_in, transfer, coupling, far_in)])

    def up4(own, masks, axis, copies, *behind):
        got = [swap(own, masks[i - 1]) for i in ORDER]
        top = of((copies,) + pair.shape, F32) if copies else pair
        return pl.pallas_call(
            lambda *refs: up4_kernel(copies, axis, refs),
            out_shape=(mat(12), top), in_specs=[VMEM] * (5 + len(behind)), out_specs=(VMEM,) * 2,
            scratch_shapes=[pltpu.VMEM((4,) + pair.shape, F32)], name="up4", compiler_params=PARAMS,
        )(own, *got, tsplit, *behind)

    def up2(own, mask, axis, *sources):
        return pl.pallas_call(
            lambda *refs: up2_kernel(axis, refs),
            out_shape=(mat(4), pair, of((2,) + src_in.shape, BF16)), in_specs=[VMEM] * 6, out_specs=(VMEM,) * 3,
            scratch_shapes=[pltpu.VMEM((2,) + pair.shape, F32)], name="up2", compiler_params=PARAMS,
        )(own, swap(own, mask), tsplit, *sources)

    loc_a, top = pl.pallas_call(
        low_kernel, out_shape=(mat(4), of((2, 16 * rank, rank), BF16)), in_specs=[VMEM] * 4, out_specs=(VMEM,) * 2,
        scratch_shapes=[pltpu.VMEM((4, rank, rank), F32)] * 3,
        name="low", compiler_params=PARAMS,
    )(far, coup, tsplit, m1)
    core, cross4 = swap(src, 4), swap_across(src, 4)
    m23, pair4 = up4(pair2, (1, 2, 3), "x", 0, loc_a)
    m4, pair5, both = up2(pair4, 4, "c", src, cross4, core)
    loc_b = pl.pallas_call(
        low2_kernel, out_shape=mat(12), in_specs=[VMEM] * 6, out_specs=VMEM,
        name="low2", compiler_params=PARAMS,
    )(far, coup, m0, m23, m4, pair5)

    shifted = shift(both)
    m56, pair7 = up4(pair5, (8, 16, 24), "y", 8, loc_b)
    g7 = lax.all_to_all(pair7, "z", 0, 0, tiled=True)
    other = swap(shifted[1], 4)

    far_part, g, blocks = pl.pallas_call(
        mid_kernel,
        out_shape=(of((rhs, points), F32), of((2, rhs, points), BF16), of(near_blocks.shape, BF16)),
        in_specs=[VMEM] * 6 + [HBM] * 2, out_specs=(VMEM,) * 3,
        scratch_shapes=[pltpu.VMEM(basis_in.shape, BF16), pltpu.SemaphoreType.DMA((2,))],
        name="mid", compiler_params=PARAMS,
    )(far, coup, tsplit, loc_a, loc_b, m56, in_hbm(basis_in), in_hbm(near_blocks))
    part = pl.pallas_call(
        near_kernel,
        out_shape=of((rhs, points), F32),
        in_specs=[VMEM] * 6 + [HBM] * 2, out_specs=VMEM,
        scratch_shapes=[
            pltpu.VMEM((5 * leaves, rhs, pts), BF16),
            pltpu.VMEM(src_in.shape, BF16),
            pltpu.SMEM(near_pattern.shape[::-1], jnp.int32),
            pltpu.SemaphoreType.DMA((2,)),
        ],
        name="near", compiler_params=PARAMS,
    )(far_part, core, cross4, shifted, other, blocks, in_hbm(src_in), in_hbm(near_pattern.T))

    product = pl.pallas_call(
        last_kernel,
        out_shape=of((rhs, points), BF16),
        in_specs=[VMEM] * 4, out_specs=VMEM,
        name="last", compiler_params=PARAMS,
    )(top, g7, part, g)
    return product.T


def solution(mesh):
    leaf, sub = mesh.shape["leaf"], mesh.shape["sub"]
    cut = Mesh(mesh.devices.reshape(leaf // 8, 4, 2, sub), AXES)
    placed = (
        P(AXES, None),
        P(AXES, None, None),
        P(),
        P(),
        P(AXES, None, None, None),
        P(AXES, None),
        P(),
    )
    return jax.shard_map(shards, mesh=cut, in_specs=placed, out_specs=P(AXES, None), check_vma=False)
```

```python
import jax
import jax.numpy as jnp
from jax import lax
from jax.experimental import pallas as pl
from jax.experimental.pallas import tpu as pltpu
from jax.sharding import Mesh, PartitionSpec as P

AXES = ("z", "y", "c", "x")
F32 = jnp.float32
BF16 = jnp.bfloat16
NN = (((1,), (0,)), ((), ()))
NT = (((1,), (1,)), ((), ()))
VMEM = pl.BlockSpec(memory_space=pltpu.VMEM)
SMEM = pl.BlockSpec(memory_space=pltpu.SMEM)
HBM = pl.BlockSpec(memory_space=pltpu.HBM)
ORDER = (2, 1, 3)
PARAMS = pltpu.CompilerParams(vmem_limit_bytes=4 * 1024 * 1024)


def in_hbm(array):
    return pltpu.with_memory_space_constraint(array, pltpu.HBM)


def split(a):
    high = a.astype(BF16)
    return high, (a - high.astype(F32)).astype(BF16)


def dot(a, b, dims):
    return lax.dot_general(a, b, dims, preferred_element_type=F32)


def dot3(a, b, dims):
    return dot(a[0], b[0], dims) + (dot(a[0], b[1], dims) + dot(a[1], b[0], dims))


def lift(pairs, tsplit):
    return dot3(split(pairs), (tsplit[0], tsplit[1]), NN)


def child_transfer(tsplit, child):
    at = pl.ds(pl.multiple_of(child * 64, 64), 64)
    return tsplit[0, at], tsplit[1, at]


def paired(values):
    whole = [values[i * 64 : (i + 1) * 64] for i in range(values.shape[0] // 64)]
    return jnp.concatenate([pair_of(whole[i], whole[i + 1]) for i in range(0, len(whole), 2)], axis=0)


def pair_of(first, second):
    return jnp.concatenate([first, second], axis=1)


def device_index():
    z, y, c, x = (lax.axis_index(a) for a in AXES)
    return ((z * lax.axis_size("y") + y) * lax.axis_size("c") + c) * lax.axis_size("x") + x


def device_count():
    count = 1
    for a in AXES:
        count *= lax.axis_size(a)
    return count


def swap(array, mask):
    return lax.ppermute(array, AXES, [(i, i ^ mask) for i in range(device_count())])


def across(device, step, count):
    return (device + jnp.where(device & step, step, count - step)) % count


def swap_across(array, step):
    n = device_count()
    others = [i + step if i & step else i - step for i in range(n)]
    return lax.ppermute(array, AXES, [(i, o if 0 <= o < n else i ^ 1) for i, o in enumerate(others)])


def shift(array):
    n, span = device_count(), lax.axis_size("x")
    step = lambda i: -1 if i // span % 2 else 1
    return lax.ppermute(array, AXES, [(i, i // span * span + (i + step(i)) % span) for i in range(n)])


def leaf_kernel(src_in, basis_in, transfer_in, coupling_in, far_in, src, coupling, far, tsplit, m0, m1, pair2, basis, raw, sems):
    copies = [
        pltpu.make_async_copy(a, b, sems.at[i])
        for i, (a, b) in enumerate(
            ((src_in, src), (basis_in, basis), (transfer_in, raw), (coupling_in, coupling), (far_in, far))
        )
    ]
    for copy in copies:
        copy.start()
    for copy in copies[:3]:
        copy.wait()
    for i in range(2):
        tsplit[0, i * 64 : (i + 1) * 64], tsplit[1, i * 64 : (i + 1) * 64] = split(raw[i])
    leaves, _, pts = basis.shape
    low = []
    for i in range(leaves):
        v = dot(src[:, i * pts : (i + 1) * pts], basis[i], NT)
        m0[i] = v
        low.append(v)
    mid = lift(paired(jnp.concatenate(low, axis=0)), tsplit)
    for i in range(leaves // 2):
        m1[i] = mid[i * 64 : (i + 1) * 64]
    pair2[...] = paired(lift(paired(mid), tsplit))
    for copy in copies[3:]:
        copy.wait()


def clusters(pairs, out):
    for i, p in enumerate(pairs):
        out[2 * i] = p[:, :64]
        out[2 * i + 1] = p[:, 64:]


def up4_kernel(copies, axis, refs):
    own, p1, p2, p3, tsplit = refs[:5]
    ab, pair, ordered = refs[-3:]
    here = lax.axis_index(axis)
    for i, ref in zip((0,) + ORDER, (own, p1, p2, p3)):
        ordered[here ^ i] = ref[...]
    clusters([ordered[i] for i in range(4)], ab)
    mid = lift(jnp.concatenate([ordered[i] for i in range(4)], axis=0), tsplit)
    for i in range(4):
        ab[8 + i] = mid[i * 64 : (i + 1) * 64]
    top = paired(lift(paired(mid), tsplit))
    if copies:
        onward = refs[5]
        sent = dot3(split(top), (onward[0], onward[1]), NN)
        for i in range(copies):
            one = sent[:, i * 64 : (i + 1) * 64]
            pair[i] = pair_of(one[:32], one[32:])
    else:
        pair[...] = top


def up2_kernel(axis, refs):
    own, p1, tsplit, src, cross4, core = refs[:6]
    a, pair, both, ordered = refs[-4:]
    here = lax.axis_index(axis)
    for i, ref in enumerate((own, p1)):
        ordered[here ^ i] = ref[...]
    clusters([ordered[i] for i in range(2)], a)
    pair[...] = paired(lift(jnp.concatenate([ordered[i] for i in range(2)], axis=0), tsplit))
    c, x = lax.axis_index("c"), lax.axis_index("x")
    end = x == jnp.where(c == 0, lax.axis_size("x") - 1, 0)

    @pl.when(end)
    def _():
        both[0] = cross4[...]
        both[1] = src[...]

    @pl.when(jnp.logical_not(end))
    def _():
        both[0] = src[...]
        both[1] = core[...]


def start_of(level):
    return sum(2048 >> l for l in range(level))


def weights_of(far, level, cluster):
    row = start_of(level) + cluster
    total = far.shape[1]
    tail = total // 128 * 128
    if start_of(level) >= tail:
        chunk, base = far[:, tail:], tail
    else:
        base = row // 128 * 128
        chunk = far[:, pl.ds(pl.multiple_of(base, 128), 128)]
    lane = lax.broadcasted_iota(jnp.int32, chunk.shape, 1)
    w = jnp.sum(jnp.where(lane == row - base, chunk, 0), axis=1, keepdims=True).astype(F32)
    return [w[j : j + 1, :] for j in range(3)]


def weight_at(far, level, cluster, offset):
    row = start_of(level) + cluster
    total = far.shape[1]
    tail = total // 128 * 128
    if start_of(level) >= tail:
        chunk, base = far[:, tail:], tail
    else:
        base = row // 128 * 128
        chunk = far[:, pl.ds(pl.multiple_of(base, 128), 128)]
    lane = lax.broadcasted_iota(jnp.int32, chunk.shape, 1)
    which = lax.broadcasted_iota(jnp.int32, chunk.shape, 0)
    found = jnp.where((lane == row - base) & (which == offset - 1), chunk, 0)
    return jnp.sum(jnp.sum(found, axis=1, keepdims=True), axis=0, keepdims=True).astype(F32)


def couple(weights, sources, coupling):
    total = None
    for w, m, c in zip(weights, sources, coupling):
        term = dot3(split(m * w), c, NT)
        total = term if total is None else total + term
    return total


def local(far, c, level, cluster, values, width, first=0):
    at = cluster % width
    group = at // 4 * 4 + first
    return couple(weights_of(far, level, cluster), [values[group + (at + j) % 4] for j in (1, 2, 3)], c)


def low_kernel(far, coupling, tsplit, m1, loc_a, top, d7, d8, d9):
    c = [split(coupling[i]) for i in range(3)]
    d = device_index()
    for i in range(4):
        w = weights_of(far, 1, d * 4 + i)
        loc_a[i] = couple(w, [m1[(i + j) % 4] for j in (1, 2, 3)], c)

    z, half, planes = lax.axis_index("z"), lax.axis_index("y") >> 1, lax.axis_size("z")
    turned = jnp.concatenate([coupling[i].T for i in range(3)], axis=0)
    below = child_transfer(tsplit, half)
    parts = split(turned)
    above = [dot3(parts, child_transfer(tsplit, k), NT) for k in (0, 1)]
    from8 = dot3(parts, below, NT)
    from9 = dot3(split(jnp.concatenate(above, axis=0)), below, NT)
    for held, values in ((d7, turned), (d8, from8), (d9, from9)):
        for j in range(values.shape[0] // 64):
            held[j] = values[j * 64 : (j + 1) * 64]

    def term(held, first, level, target, source):
        offset = (source - target) & 3
        w = weight_at(far, level, target, offset) * jnp.where(source >> 2 == target >> 2, 1.0, 0.0)
        return w * held[first + jnp.maximum(offset - 1, 0)]

    whole = jnp.concatenate([term(d9, p % 2 * 3, 9, p >> 1, z >> 1) for p in range(planes)], axis=1)
    whole = dot3(child_transfer(tsplit, z & 1), split(whole), NN)
    whole = whole + jnp.concatenate([term(d8, 0, 8, p, z) for p in range(planes)], axis=1)
    whole = dot3((tsplit[0], tsplit[1]), split(whole), NN)
    own = [
        jnp.concatenate([term(d7, 0, 7, 2 * p + half, 2 * z + k) for p in range(planes)], axis=1) for k in (0, 1)
    ]
    top[0], top[1] = split(whole + jnp.concatenate(own, axis=0))


def low2_kernel(far, coupling, m0, m23, m4, behind, loc_b):
    c = [split(coupling[i]) for i in range(3)]
    d = device_index()
    for i in range(8):
        w = weights_of(far, 0, d * 8 + i)
        loc_b[4 + i] = couple(w, [m0[i // 4 * 4 + (i + j) % 4] for j in (1, 2, 3)], c)
    for i in range(2):
        loc_b[i] = local(far, c, 2, d * 2 + i, m23, 8)
    loc_b[2] = local(far, c, 3, d, m23, 4, 8)
    loc_b[3] = local(far, c, 4, d >> 1, m4, 4)


def mid_kernel(far, coupling, tsplit, loc_a, loc_b, m56, basis_in, blocks_in, part, g, blocks, basis, sems):
    basis_copy = pltpu.make_async_copy(basis_in, basis, sems.at[0])
    basis_copy.start()
    blocks_copy = pltpu.make_async_copy(blocks_in, blocks, sems.at[1])
    blocks_copy.start()
    c = [split(coupling[i]) for i in range(3)]
    d = device_index()
    rows = lax.broadcasted_iota(jnp.int32, (64, 64), 0)
    cols = lax.broadcasted_iota(jnp.int32, (64, 64), 1)
    chain = jnp.where(rows == cols, 1.0, 0.0).astype(F32)
    zero = jnp.zeros((64, 64), F32)
    state = jnp.concatenate([zero, chain], 0)
    for level, width, first in ((6, 4, 8), (5, 8, 0), (4, 0, 0), (3, 0, 0)):
        cluster = d >> (level - 3)
        here = local(far, c, level, cluster, m56, width, first) if width else loc_b[level - 1]
        state = dot3(split(state), child_transfer(tsplit, cluster % 2), NT) + jnp.concatenate([here, zero], 0)
    for locs, first, count in ((loc_b, 0, 2), (loc_a, 0, 4), (loc_b, 4, 8)):
        parts = split(state)
        sides = [dot3(parts, (tsplit[0, k * 64 : (k + 1) * 64], tsplit[1, k * 64 : (k + 1) * 64]), NT) for k in (0, 1)]
        below = []
        for i in range(count):
            at = i // 2 * 128
            below.append(sides[i % 2][at : at + 64] + locs[first + i])
            below.append(sides[i % 2][at + 64 : at + 128])
        state = jnp.concatenate(below, 0)
    basis_copy.wait()
    leaves, _, pts = basis.shape
    high, low = split(state)
    for i in range(leaves):
        rows_at = slice(i * 128, (i + 1) * 128)
        at = slice(i * pts, (i + 1) * pts)
        whole = dot(high[rows_at], basis[i], NN) + dot(low[rows_at], basis[i], NN)
        part[:, at] = whole[:64]
        g[0, :, at], g[1, :, at] = split(whole[64:])
    blocks_copy.wait()


def near_kernel(far_part, core, cross4, shifted, other, blocks, src_in, pattern_in, part, held, own, pattern, sems):
    leaves, slots, pts = blocks.shape[:3]
    own_copy = pltpu.make_async_copy(src_in, own, sems.at[0])
    own_copy.start()
    pattern_copy = pltpu.make_async_copy(pattern_in, pattern, sems.at[1])
    pattern_copy.start()
    for n, ref in enumerate((core, cross4, shifted.at[0], other)):
        for i in range(leaves):
            held[(n + 1) * leaves + i] = ref[:, i * pts : (i + 1) * pts]
    own_copy.wait()
    for i in range(leaves):
        held[i] = own[:, i * pts : (i + 1) * pts]
    pattern_copy.wait()
    d = device_index()
    others = [d, d ^ 4, across(d, 4, device_count()), d + jnp.where(lax.axis_index("c") == 0, -1, 1)]
    for i in range(leaves):
        at = slice(i * pts, (i + 1) * pts)
        total = far_part[:, at]
        for s in range(slots):
            j = pattern[s, i]
            device = j // leaves
            slot = jnp.int32(4)
            for k, other_device in enumerate(others):
                slot = jnp.where(device == other_device, k, slot)
            total = total + dot(held[slot * leaves + j % leaves], blocks[i, s], NT)
        part[:, at] = total


def last_kernel(g7, part, g, out):
    total = g7[0]
    for i in range(1, g7.shape[0]):
        total = total + g7[i]
    field = jnp.concatenate([total[:, :64], total[:, 64:]], axis=0)
    high, low = split(field)
    both = jnp.concatenate([high, low], 0)
    step = 256
    for at in range(0, out.shape[1], step):
        at = slice(at, at + step)
        first = dot(both, g[0, :, at], NN)
        far_part = first[:64] + (first[64:] + dot(high, g[1, :, at], NN))
        out[:, at] = (far_part + part[:, at]).astype(BF16)


def shards(sources, leaf_basis, transfer, coupling, near_blocks, near_pattern, far_pattern):
    leaves, pts, rank = leaf_basis.shape
    rhs = sources.shape[1]
    points = leaves * pts
    src_in = sources.T
    basis_in = jnp.swapaxes(leaf_basis, 1, 2)
    far_in = far_pattern.T
    of = jax.ShapeDtypeStruct
    mat = lambda n: of((n, rhs, rank), F32)
    pair = of((rhs, 2 * rank), F32)

    src, coup, far, tsplit, m0, m1, pair2 = pl.pallas_call(
        leaf_kernel,
        out_shape=(
            of(src_in.shape, BF16), of(coupling.shape, F32), of(far_in.shape, jnp.int32),
            of((2, 2 * rank, rank), BF16), mat(8), mat(4), pair,
        ),
        in_specs=[HBM] * 5, out_specs=(VMEM,) * 7,
        scratch_shapes=[pltpu.VMEM(basis_in.shape, BF16), pltpu.VMEM(transfer.shape, F32), pltpu.SemaphoreType.DMA((5,))],
        name="leaf", compiler_params=PARAMS,
    )(*[in_hbm(a) for a in (src_in, basis_in, transfer, coupling, far_in)])

    def up4(own, masks, axis, copies, *behind):
        got = [swap(own, masks[i - 1]) for i in ORDER]
        top = of((copies, rhs // 2, 2 * rank), F32) if copies else pair
        return pl.pallas_call(
            lambda *refs: up4_kernel(copies, axis, refs),
            out_shape=(mat(12), top), in_specs=[VMEM] * (5 + len(behind)), out_specs=(VMEM,) * 2,
            scratch_shapes=[pltpu.VMEM((4,) + pair.shape, F32)], name="up4", compiler_params=PARAMS,
        )(own, *got, tsplit, *behind)

    def up2(own, mask, axis, *sources):
        return pl.pallas_call(
            lambda *refs: up2_kernel(axis, refs),
            out_shape=(mat(4), pair, of((2,) + src_in.shape, BF16)), in_specs=[VMEM] * 6, out_specs=(VMEM,) * 3,
            scratch_shapes=[pltpu.VMEM((2,) + pair.shape, F32)], name="up2", compiler_params=PARAMS,
        )(own, swap(own, mask), tsplit, *sources)

    loc_a, top = pl.pallas_call(
        low_kernel, out_shape=(mat(4), of((2, 2 * rank, lax.axis_size("z") * rank), BF16)), in_specs=[VMEM] * 4, out_specs=(VMEM,) * 2,
        scratch_shapes=[pltpu.VMEM((n, rank, rank), F32) for n in (3, 3, 6)],
        name="low", compiler_params=PARAMS,
    )(far, coup, tsplit, m1)
    core, cross4 = swap(src, 4), swap_across(src, 4)
    m23, pair4 = up4(pair2, (1, 2, 3), "x", 0, loc_a)
    m4, pair5, both = up2(pair4, 4, "c", src, cross4, core)
    loc_b = pl.pallas_call(
        low2_kernel, out_shape=mat(12), in_specs=[VMEM] * 6, out_specs=VMEM,
        name="low2", compiler_params=PARAMS,
    )(far, coup, m0, m23, m4, pair5)

    shifted = shift(both)
    m56, pair7 = up4(pair5, (8, 16, 24), "y", lax.axis_size("z"), top, loc_b)
    g7 = lax.all_to_all(pair7, "z", 0, 0, tiled=True)
    late = lax.optimization_barrier((shifted, m56))[0]
    other = swap(late[1], 4)

    far_part, g, blocks = pl.pallas_call(
        mid_kernel,
        out_shape=(of((rhs, points), F32), of((2, rhs, points), BF16), of(near_blocks.shape, BF16)),
        in_specs=[VMEM] * 6 + [HBM] * 2, out_specs=(VMEM,) * 3,
        scratch_shapes=[pltpu.VMEM(basis_in.shape, BF16), pltpu.SemaphoreType.DMA((2,))],
        name="mid", compiler_params=PARAMS,
    )(far, coup, tsplit, loc_a, loc_b, m56, in_hbm(basis_in), in_hbm(near_blocks))
    part = pl.pallas_call(
        near_kernel,
        out_shape=of((rhs, points), F32),
        in_specs=[VMEM] * 6 + [HBM] * 2, out_specs=VMEM,
        scratch_shapes=[
            pltpu.VMEM((5 * leaves, rhs, pts), BF16),
            pltpu.VMEM(src_in.shape, BF16),
            pltpu.SMEM(near_pattern.shape[::-1], jnp.int32),
            pltpu.SemaphoreType.DMA((2,)),
        ],
        name="near", compiler_params=PARAMS,
    )(far_part, core, cross4, shifted, other, blocks, in_hbm(src_in), in_hbm(near_pattern.T))

    product = pl.pallas_call(
        last_kernel,
        out_shape=of((rhs, points), BF16),
        in_specs=[VMEM] * 3, out_specs=VMEM,
        name="last", compiler_params=PARAMS,
    )(g7, part, g)
    return product.T


def solution(mesh):
    leaf, sub = mesh.shape["leaf"], mesh.shape["sub"]
    cut = Mesh(mesh.devices.reshape(leaf // 8, 4, 2, sub), AXES)
    placed = (
        P(AXES, None),
        P(AXES, None, None),
        P(),
        P(),
        P(AXES, None, None, None),
        P(AXES, None),
        P(),
    )
    return jax.shard_map(shards, mesh=cut, in_specs=placed, out_specs=P(AXES, None), check_vma=False)
```

```python
import jax
import jax.numpy as jnp
from jax import lax
from jax.experimental import pallas as pl
from jax.experimental.pallas import tpu as pltpu
from jax.sharding import Mesh, PartitionSpec as P

AXES = ("z", "y", "c", "x")
F32 = jnp.float32
BF16 = jnp.bfloat16
NN = (((1,), (0,)), ((), ()))
NT = (((1,), (1,)), ((), ()))
VMEM = pl.BlockSpec(memory_space=pltpu.VMEM)
SMEM = pl.BlockSpec(memory_space=pltpu.SMEM)
HBM = pl.BlockSpec(memory_space=pltpu.HBM)
ORDER = (2, 1, 3)
PARAMS = pltpu.CompilerParams(vmem_limit_bytes=4 * 1024 * 1024)


def in_hbm(array):
    return pltpu.with_memory_space_constraint(array, pltpu.HBM)


def split(a):
    high = a.astype(BF16)
    return high, (a - high.astype(F32)).astype(BF16)


def dot(a, b, dims):
    return lax.dot_general(a, b, dims, preferred_element_type=F32)


def dot3(a, b, dims):
    return dot(a[0], b[0], dims) + (dot(a[0], b[1], dims) + dot(a[1], b[0], dims))


def lift(pairs, tsplit):
    return dot3(split(pairs), (tsplit[0], tsplit[1]), NN)


def child_transfer(tsplit, child):
    at = pl.ds(pl.multiple_of(child * 64, 64), 64)
    return tsplit[0, at], tsplit[1, at]


def paired(values):
    whole = [values[i * 64 : (i + 1) * 64] for i in range(values.shape[0] // 64)]
    return jnp.concatenate([pair_of(whole[i], whole[i + 1]) for i in range(0, len(whole), 2)], axis=0)


def pair_of(first, second):
    return jnp.concatenate([first, second], axis=1)


def device_index():
    z, y, c, x = (lax.axis_index(a) for a in AXES)
    return ((z * lax.axis_size("y") + y) * lax.axis_size("c") + c) * lax.axis_size("x") + x


def device_count():
    count = 1
    for a in AXES:
        count *= lax.axis_size(a)
    return count


def swap(array, mask):
    return lax.ppermute(array, AXES, [(i, i ^ mask) for i in range(device_count())])


def across(device, step, count):
    return (device + jnp.where(device & step, step, count - step)) % count


def swap_across(array, step):
    n = device_count()
    others = [i + step if i & step else i - step for i in range(n)]
    return lax.ppermute(array, AXES, [(i, o if 0 <= o < n else i ^ 1) for i, o in enumerate(others)])


def shift(array):
    n, span = device_count(), lax.axis_size("x")
    step = lambda i: -1 if i // span % 2 else 1
    return lax.ppermute(array, AXES, [(i, i // span * span + (i + step(i)) % span) for i in range(n)])


def leaf_kernel(src_in, basis_in, transfer_in, coupling_in, far_in, src, coupling, far, tsplit, m0, m1, pair2, basis, raw, sems):
    copies = [
        pltpu.make_async_copy(a, b, sems.at[i])
        for i, (a, b) in enumerate(
            ((src_in, src), (basis_in, basis), (transfer_in, raw), (coupling_in, coupling), (far_in, far))
        )
    ]
    for copy in copies:
        copy.start()
    for copy in copies[:3]:
        copy.wait()
    for i in range(2):
        tsplit[0, i * 64 : (i + 1) * 64], tsplit[1, i * 64 : (i + 1) * 64] = split(raw[i])
    leaves, _, pts = basis.shape
    low = []
    for i in range(leaves):
        v = dot(src[:, i * pts : (i + 1) * pts], basis[i], NT)
        m0[i] = v
        low.append(v)
    mid = lift(paired(jnp.concatenate(low, axis=0)), tsplit)
    for i in range(leaves // 2):
        m1[i] = mid[i * 64 : (i + 1) * 64]
    pair2[...] = paired(lift(paired(mid), tsplit))
    for copy in copies[3:]:
        copy.wait()


def clusters(pairs, out):
    for i, p in enumerate(pairs):
        out[2 * i] = p[:, :64]
        out[2 * i + 1] = p[:, 64:]


def up4_kernel(copies, axis, refs):
    own, p1, p2, p3, tsplit = refs[:5]
    ab, pair, ordered = refs[-3:]
    here = lax.axis_index(axis)
    for i, ref in zip((0,) + ORDER, (own, p1, p2, p3)):
        ordered[here ^ i] = ref[...]
    clusters([ordered[i] for i in range(4)], ab)
    mid = lift(jnp.concatenate([ordered[i] for i in range(4)], axis=0), tsplit)
    for i in range(4):
        ab[8 + i] = mid[i * 64 : (i + 1) * 64]
    top = paired(lift(paired(mid), tsplit))
    if copies:
        for i in range(copies):
            pair[i] = top
    else:
        pair[...] = top


def up2_kernel(axis, refs):
    own, p1, tsplit, src, cross4, core = refs[:6]
    a, pair, both, ordered = refs[-4:]
    here = lax.axis_index(axis)
    for i, ref in enumerate((own, p1)):
        ordered[here ^ i] = ref[...]
    clusters([ordered[i] for i in range(2)], a)
    pair[...] = paired(lift(jnp.concatenate([ordered[i] for i in range(2)], axis=0), tsplit))
    c, x = lax.axis_index("c"), lax.axis_index("x")
    end = x == jnp.where(c == 0, lax.axis_size("x") - 1, 0)

    @pl.when(end)
    def _():
        both[0] = cross4[...]
        both[1] = src[...]

    @pl.when(jnp.logical_not(end))
    def _():
        both[0] = src[...]
        both[1] = core[...]


def start_of(level):
    return sum(2048 >> l for l in range(level))


def weights_of(far, level, cluster):
    row = start_of(level) + cluster
    total = far.shape[1]
    tail = total // 128 * 128
    if start_of(level) >= tail:
        chunk, base = far[:, tail:], tail
    else:
        base = row // 128 * 128
        chunk = far[:, pl.ds(pl.multiple_of(base, 128), 128)]
    lane = lax.broadcasted_iota(jnp.int32, chunk.shape, 1)
    w = jnp.sum(jnp.where(lane == row - base, chunk, 0), axis=1, keepdims=True).astype(F32)
    return [w[j : j + 1, :] for j in range(3)]


def couple(weights, sources, coupling):
    total = None
    for w, m, c in zip(weights, sources, coupling):
        term = dot3(split(m * w), c, NT)
        total = term if total is None else total + term
    return total


def local(far, c, level, cluster, values, width, first=0):
    at = cluster % width
    group = at // 4 * 4 + first
    return couple(weights_of(far, level, cluster), [values[group + (at + j) % 4] for j in (1, 2, 3)], c)


def low_kernel(far, coupling, tsplit, m1, loc_a, top, d7, d8, d9):
    c = [split(coupling[i]) for i in range(3)]
    d = device_index()
    for i in range(4):
        w = weights_of(far, 1, d * 4 + i)
        loc_a[i] = couple(w, [m1[(i + j) % 4] for j in (1, 2, 3)], c)

    at7, at8, at9 = d >> 4, d >> 5, d >> 6
    turned = jnp.concatenate([coupling[i].T for i in range(3)], axis=0)
    below8 = child_transfer(tsplit, at8 % 2)
    below7 = child_transfer(tsplit, at7 % 2)
    from8 = dot3(split(turned), below7, NT)
    from9 = dot3(split(dot3(split(turned), below8, NT)), below7, NT)
    for held, values, level, at in ((d7, turned, 7, at7), (d8, from8, 8, at8), (d9, from9, 9, at9)):
        w = weights_of(far, level, at)
        held[0] = jnp.zeros((64, 64), F32)
        for j in (1, 2, 3):
            held[j] = w[j - 1] * values[(j - 1) * 64 : j * 64]
    lifts = (tsplit[0], tsplit[1])
    whole = jnp.concatenate([d9[(p - at9) & 3] for p in range(4)], axis=1)
    for count, held, at in ((8, d8, at8), (16, d7, at7)):
        both = dot3(lifts, split(whole), NN)
        parts = []
        for p in range(count):
            own = held[(p - at) & 3] * jnp.where(p >> 2 == at >> 2, 1.0, 0.0)
            half, column = p % 2 * 64, p // 2 * 64
            parts.append(both[half : half + 64, column : column + 64] + own)
        whole = jnp.concatenate(parts, axis=1) if count == 8 else jnp.concatenate(parts, axis=0)
    top[0], top[1] = split(whole)


def low2_kernel(far, coupling, m0, m23, m4, behind, loc_b):
    c = [split(coupling[i]) for i in range(3)]
    d = device_index()
    for i in range(8):
        w = weights_of(far, 0, d * 8 + i)
        loc_b[4 + i] = couple(w, [m0[i // 4 * 4 + (i + j) % 4] for j in (1, 2, 3)], c)
    for i in range(2):
        loc_b[i] = local(far, c, 2, d * 2 + i, m23, 8)
    loc_b[2] = local(far, c, 3, d, m23, 4, 8)
    loc_b[3] = local(far, c, 4, d >> 1, m4, 4)


def mid_kernel(far, coupling, tsplit, loc_a, loc_b, m56, basis_in, blocks_in, part, g, blocks, basis, sems):
    basis_copy = pltpu.make_async_copy(basis_in, basis, sems.at[0])
    basis_copy.start()
    blocks_copy = pltpu.make_async_copy(blocks_in, blocks, sems.at[1])
    blocks_copy.start()
    c = [split(coupling[i]) for i in range(3)]
    d = device_index()
    rows = lax.broadcasted_iota(jnp.int32, (64, 64), 0)
    cols = lax.broadcasted_iota(jnp.int32, (64, 64), 1)
    chain = jnp.where(rows == cols, 1.0, 0.0).astype(F32)
    zero = jnp.zeros((64, 64), F32)
    state = jnp.concatenate([zero, chain], 0)
    for level, width, first in ((6, 4, 8), (5, 8, 0), (4, 0, 0), (3, 0, 0)):
        cluster = d >> (level - 3)
        here = local(far, c, level, cluster, m56, width, first) if width else loc_b[level - 1]
        state = dot3(split(state), child_transfer(tsplit, cluster % 2), NT) + jnp.concatenate([here, zero], 0)
    for locs, first, count in ((loc_b, 0, 2), (loc_a, 0, 4), (loc_b, 4, 8)):
        parts = split(state)
        sides = [dot3(parts, (tsplit[0, k * 64 : (k + 1) * 64], tsplit[1, k * 64 : (k + 1) * 64]), NT) for k in (0, 1)]
        below = []
        for i in range(count):
            at = i // 2 * 128
            below.append(sides[i % 2][at : at + 64] + locs[first + i])
            below.append(sides[i % 2][at + 64 : at + 128])
        state = jnp.concatenate(below, 0)
    basis_copy.wait()
    leaves, _, pts = basis.shape
    high, low = split(state)
    for i in range(leaves):
        rows_at = slice(i * 128, (i + 1) * 128)
        at = slice(i * pts, (i + 1) * pts)
        whole = dot(high[rows_at], basis[i], NN) + dot(low[rows_at], basis[i], NN)
        part[:, at] = whole[:64]
        g[0, :, at], g[1, :, at] = split(whole[64:])
    blocks_copy.wait()


def near_kernel(far_part, core, cross4, shifted, other, blocks, src_in, pattern_in, part, held, own, pattern, sems):
    leaves, slots, pts = blocks.shape[:3]
    own_copy = pltpu.make_async_copy(src_in, own, sems.at[0])
    own_copy.start()
    pattern_copy = pltpu.make_async_copy(pattern_in, pattern, sems.at[1])
    pattern_copy.start()
    for n, ref in enumerate((core, cross4, shifted.at[0], other)):
        for i in range(leaves):
            held[(n + 1) * leaves + i] = ref[:, i * pts : (i + 1) * pts]
    own_copy.wait()
    for i in range(leaves):
        held[i] = own[:, i * pts : (i + 1) * pts]
    pattern_copy.wait()
    d = device_index()
    others = [d, d ^ 4, across(d, 4, device_count()), d + jnp.where(lax.axis_index("c") == 0, -1, 1)]
    for i in range(leaves):
        at = slice(i * pts, (i + 1) * pts)
        total = far_part[:, at]
        for s in range(slots):
            j = pattern[s, i]
            device = j // leaves
            slot = jnp.int32(4)
            for k, other_device in enumerate(others):
                slot = jnp.where(device == other_device, k, slot)
            total = total + dot(held[slot * leaves + j % leaves], blocks[i, s], NT)
        part[:, at] = total


def last_kernel(top, g7, part, g, out):
    moments = jnp.concatenate([g7[i] for i in range(8)], axis=1)
    field = dot3(split(moments), (top[0], top[1]), NN)
    high, low = split(field)
    both = jnp.concatenate([high, low], 0)
    step = 256
    for at in range(0, out.shape[1], step):
        at = slice(at, at + step)
        first = dot(both, g[0, :, at], NN)
        far_part = first[:64] + (first[64:] + dot(high, g[1, :, at], NN))
        out[:, at] = (far_part + part[:, at]).astype(BF16)


def shards(sources, leaf_basis, transfer, coupling, near_blocks, near_pattern, far_pattern):
    leaves, pts, rank = leaf_basis.shape
    rhs = sources.shape[1]
    points = leaves * pts
    src_in = sources.T
    basis_in = jnp.swapaxes(leaf_basis, 1, 2)
    far_in = far_pattern.T
    of = jax.ShapeDtypeStruct
    mat = lambda n: of((n, rhs, rank), F32)
    pair = of((rhs, 2 * rank), F32)

    src, coup, far, tsplit, m0, m1, pair2 = pl.pallas_call(
        leaf_kernel,
        out_shape=(
            of(src_in.shape, BF16), of(coupling.shape, F32), of(far_in.shape, jnp.int32),
            of((2, 2 * rank, rank), BF16), mat(8), mat(4), pair,
        ),
        in_specs=[HBM] * 5, out_specs=(VMEM,) * 7,
        scratch_shapes=[pltpu.VMEM(basis_in.shape, BF16), pltpu.VMEM(transfer.shape, F32), pltpu.SemaphoreType.DMA((5,))],
        name="leaf", compiler_params=PARAMS,
    )(*[in_hbm(a) for a in (src_in, basis_in, transfer, coupling, far_in)])

    def up4(own, masks, axis, copies, *behind):
        got = [swap(own, masks[i - 1]) for i in ORDER]
        top = of((copies,) + pair.shape, F32) if copies else pair
        return pl.pallas_call(
            lambda *refs: up4_kernel(copies, axis, refs),
            out_shape=(mat(12), top), in_specs=[VMEM] * (5 + len(behind)), out_specs=(VMEM,) * 2,
            scratch_shapes=[pltpu.VMEM((4,) + pair.shape, F32)], name="up4", compiler_params=PARAMS,
        )(own, *got, tsplit, *behind)

    def up2(own, mask, axis, *sources):
        return pl.pallas_call(
            lambda *refs: up2_kernel(axis, refs),
            out_shape=(mat(4), pair, of((2,) + src_in.shape, BF16)), in_specs=[VMEM] * 6, out_specs=(VMEM,) * 3,
            scratch_shapes=[pltpu.VMEM((2,) + pair.shape, F32)], name="up2", compiler_params=PARAMS,
        )(own, swap(own, mask), tsplit, *sources)

    loc_a, top = pl.pallas_call(
        low_kernel, out_shape=(mat(4), of((2, 16 * rank, rank), BF16)), in_specs=[VMEM] * 4, out_specs=(VMEM,) * 2,
        scratch_shapes=[pltpu.VMEM((4, rank, rank), F32)] * 3,
        name="low", compiler_params=PARAMS,
    )(far, coup, tsplit, m1)
    core, cross4 = swap(src, 4), swap_across(src, 4)
    m23, pair4 = up4(pair2, (1, 2, 3), "x", 0, loc_a)
    m4, pair5, both = up2(pair4, 4, "c", src, cross4, core)
    loc_b = pl.pallas_call(
        low2_kernel, out_shape=mat(12), in_specs=[VMEM] * 6, out_specs=VMEM,
        name="low2", compiler_params=PARAMS,
    )(far, coup, m0, m23, m4, pair5)

    shifted = shift(both)
    m56, pair7 = up4(pair5, (8, 16, 24), "y", 8, loc_b)
    g7 = lax.all_to_all(pair7, "z", 0, 0, tiled=True)
    other = swap(shifted[1], 4)

    far_part, g, blocks = pl.pallas_call(
        mid_kernel,
        out_shape=(of((rhs, points), F32), of((2, rhs, points), BF16), of(near_blocks.shape, BF16)),
        in_specs=[VMEM] * 6 + [HBM] * 2, out_specs=(VMEM,) * 3,
        scratch_shapes=[pltpu.VMEM(basis_in.shape, BF16), pltpu.SemaphoreType.DMA((2,))],
        name="mid", compiler_params=PARAMS,
    )(far, coup, tsplit, loc_a, loc_b, m56, in_hbm(basis_in), in_hbm(near_blocks))
    part = pl.pallas_call(
        near_kernel,
        out_shape=of((rhs, points), F32),
        in_specs=[VMEM] * 6 + [HBM] * 2, out_specs=VMEM,
        scratch_shapes=[
            pltpu.VMEM((5 * leaves, rhs, pts), BF16),
            pltpu.VMEM(src_in.shape, BF16),
            pltpu.SMEM(near_pattern.shape[::-1], jnp.int32),
            pltpu.SemaphoreType.DMA((2,)),
        ],
        name="near", compiler_params=PARAMS,
    )(far_part, core, cross4, shifted, other, blocks, in_hbm(src_in), in_hbm(near_pattern.T))

    product = pl.pallas_call(
        last_kernel,
        out_shape=of((rhs, points), BF16),
        in_specs=[VMEM] * 4, out_specs=VMEM,
        name="last", compiler_params=PARAMS,
    )(top, g7, part, g)
    return product.T


def solution(mesh):
    leaf, sub = mesh.shape["leaf"], mesh.shape["sub"]
    cut = Mesh(mesh.devices.reshape(leaf // 8, 4, 2, sub), AXES)
    placed = (
        P(AXES, None),
        P(AXES, None, None),
        P(),
        P(),
        P(AXES, None, None, None),
        P(AXES, None),
        P(),
    )
    return jax.shard_map(shards, mesh=cut, in_specs=placed, out_specs=P(AXES, None), check_vma=False)
```
